32 devices in a mesh: gx: 4 (over z), gy: 2 (over core), gz: 4 (over y, x).
Axes of the slice: x: 2, y: 2, z: 4, core: 2. Of those that a mesh axis runs over, the one named last changes fastest.
Arguments:
- flow_pops: float32 [19, 16, 16, 512], P(None, 'gx', 'gy', 'gz'), may hold values from 0.3 to 0.8
- phase_pops: float32 [7, 16, 16, 512], P(None, 'gx', 'gy', 'gz'), may hold values from -0.15 to 0.15
- pore_mask: int32 [16, 16, 512], P('gx', 'gy', 'gz'), may hold values from 0 to 1, as said below
Outputs:
- flow_next: float32 [19, 16, 16, 512], P(None, 'gx', 'gy', 'gz')
- phase_next: float32 [7, 16, 16, 512], P(None, 'gx', 'gy', 'gz')
The draws below stay inside these ranges and needn't reach their ends.
Inputs may be any that keep to these rules, and one draw needn't show every extreme that they name: `pore_mask`: 1 marks a pore voxel, 0 a rock voxel. Pores and rock form clusters several voxels wide, and whole aligned blocks of 4 x 8 x 128 voxels may be rock.
All inputs are finite; a program needn't handle non-finite values.
Results may differ from the reference program's by a relative error of at most 0.0003.
Values sent between devices are 32-bit elements; how exact they have to be, the bound alone decides.
No kernel may reach another device: no remote copies, remote signals or barrier semaphores. Data moves between devices by JAX's collectives and lax.ppermute only.
A program may use at most 64 MiB of HBM per device.

```python
import jax
import jax.numpy as jnp
from jax import lax

CX = 4
CY = 8
CZ = 128
STEPS = 2
QF = 19
QG = 7
NX = 16
NY = 16
NZ = 512


def draw_pore_mask(key, part):
    key_block = jax.random.fold_in(key, 11)
    key_cell = jax.random.fold_in(key, 23)
    blocks = jax.random.randint(key_block, (NX // CX, NY // CY, NZ // CZ), 0, 10)
    keep = (blocks >= 2).astype(jnp.int32)
    keep_full = jnp.repeat(jnp.repeat(jnp.repeat(keep, CX, axis=0), CY, axis=1), CZ, axis=2)
    noise = jax.random.randint(key_cell, (NX, NY, NZ), 0, 16)
    total = jnp.zeros((NX, NY, NZ), jnp.int32)
    for shift_x in (-1, 0, 1):
        for shift_y in (-1, 0, 1):
            for shift_z in (-1, 0, 1):
                total = total + jnp.roll(noise, (shift_x, shift_y, shift_z), axis=(0, 1, 2))
    pore = (total >= 190).astype(jnp.int32)
    return pore * keep_full


def block_scale(key, shape, split, smallest, top_value):
    loudness = 1.0
    for position, shards_of in split:
        steps = jax.random.uniform(jax.random.fold_in(jax.random.fold_in(key, 6), position), (shards_of,), jnp.float32, smallest / len(split), top_value / len(split))
        loudness = loudness * jnp.repeat(jnp.exp(steps), shape[position] // shards_of).reshape((-1,) + (1,) * (len(shape) - 1 - position))
    return loudness


def setup_inputs(seed: int = 0) -> dict:
    seeds = jax.random.split(jax.random.key(seed), 4)
    return {
        "flow_pops": jnp.clip(0.3 + 0.5 * jax.random.uniform(seeds[0], (QF, NX, NY, NZ), jnp.float32) ** block_scale(seeds[0], (QF, NX, NY, NZ), ((1, 4), (2, 2), (3, 4)), -0.2, 0.2), 0.3, 0.8),
        "phase_pops": jnp.clip(jax.random.uniform(seeds[1], (QG, NX, NY, NZ), jnp.float32, -0.15, 0.15) * block_scale(seeds[1], (QG, NX, NY, NZ), ((1, 4), (2, 2), (3, 4)), -0.4, 0.0), -0.15, 0.15),
        "pore_mask": draw_pore_mask(jax.random.fold_in(seeds[3], 71), 0),
    }


VEL_F = [(0, 0, 0), (1, 0, 0), (-1, 0, 0), (0, 1, 0), (0, -1, 0), (0, 0, 1), (0, 0, -1), (1, 1, 0), (-1, -1, 0), (1, -1, 0), (-1, 1, 0), (1, 0, 1), (-1, 0, -1), (1, 0, -1), (-1, 0, 1), (0, 1, 1), (0, -1, -1), (0, 1, -1), (0, -1, 1)]
OPP_F = [0, 2, 1, 4, 3, 6, 5, 8, 7, 10, 9, 12, 11, 14, 13, 16, 15, 18, 17]
WT_F = [1.0 / 3.0] + [1.0 / 18.0] * 6 + [1.0 / 36.0] * 12
BT_F = [-2.0 / 9.0] + [1.0 / 54.0] * 6 + [1.0 / 27.0] * 12
WT_G = [0.25] + [0.125] * 6
VEL_ALL = VEL_F + VEL_F[:7]
OPP_ALL = OPP_F + [19 + other for other in OPP_F[:7]]

def relax(flow_pops, phase_pops, phase, grads, fluid):
    density = sum((flow_pops[member] for member in range(19)))
    flow = [sum((VEL_F[member][dim] * flow_pops[member] for member in range(19))) / density for dim in range(3)]
    speed_sq = flow[0] * flow[0] + flow[1] * flow[1] + flow[2] * flow[2]
    omega = 1.0 / (0.8 + 0.2 * phase)
    grad_mag = jnp.sqrt(grads[0] * grads[0] + grads[1] * grads[1] + grads[2] * grads[2] + 0.01)
    results = []
    for member in range(19):
        offset = VEL_F[member]
        along = offset[0] * flow[0] + offset[1] * flow[1] + offset[2] * flow[2]
        cross = offset[0] * grads[0] + offset[1] * grads[1] + offset[2] * grads[2]
        balance = WT_F[member] * density * (1.0 + 3.0 * along + 4.5 * along * along - 1.5 * speed_sq)
        perturb = 0.5 * (WT_F[member] * cross * cross / grad_mag - BT_F[member] * grad_mag)
        relaxed = flow_pops[member] - omega * (flow_pops[member] - balance) + perturb
        results.append(jnp.where(fluid, relaxed, flow_pops[member]))
    sharpen_coef = 0.7 * (1.0 - phase * phase) / grad_mag
    for member in range(7):
        offset = VEL_F[member]
        along = offset[0] * flow[0] + offset[1] * flow[1] + offset[2] * flow[2]
        cross = offset[0] * grads[0] + offset[1] * grads[1] + offset[2] * grads[2]
        balance = WT_G[member] * (phase * (1.0 + 4.0 * along) + sharpen_coef * cross)
        relaxed = phase_pops[member] - 1.25 * (phase_pops[member] - balance)
        results.append(jnp.where(fluid, relaxed, phase_pops[member]))
    return jnp.stack(results)

def window(field, flags, offset, sizes):
    starts = [1 - offset[dim] if flags[dim] else 0 for dim in range(3)]
    return field[starts[0]:starts[0] + sizes[0], starts[1]:starts[1] + sizes[1], starts[2]:starts[2] + sizes[2]]

def propagate(post, source, fluid_pad, fluid):
    sizes = post.shape[1:]
    results = []
    for member in range(26):
        offset = VEL_ALL[member]
        field, flags = source(member)
        source_vals = window(field, flags, offset, sizes)
        source_fluid = window(fluid_pad, (1, 1, 1), offset, sizes) == 1
        moved = jnp.where(source_fluid, source_vals, post[OPP_ALL[member]])
        results.append(jnp.where(fluid, moved, post[member]))
    return jnp.stack(results)

def gradient(padded):
    grad_x = 0.5 * (padded[2:, 1:-1, 1:-1] - padded[:-2, 1:-1, 1:-1])
    grad_y = 0.5 * (padded[1:-1, 2:, 1:-1] - padded[1:-1, :-2, 1:-1])
    grad_z = 0.5 * (padded[1:-1, 1:-1, 2:] - padded[1:-1, 1:-1, :-2])
    return (grad_x, grad_y, grad_z)

def reference(flow_pops, phase_pops, pore_mask):
    fluid_pad = jnp.pad(pore_mask, 1)
    fluid = pore_mask == 1
    for step in range(STEPS):
        phase = lax.optimization_barrier(jnp.sum(phase_pops, axis=0))
        padded = jnp.pad(jnp.where(fluid, phase, jnp.float32(0.0)), 1)
        post = relax(flow_pops, phase_pops, phase, gradient(padded), fluid)
        full = jnp.pad(post, ((0, 0), (1, 1), (1, 1), (1, 1)))

        def source(member):
            return (full[member], (1, 1, 1))
        moved = propagate(post, source, fluid_pad, fluid)
        flow_pops = moved[:19]
        phase_pops = moved[19:]
    return (flow_pops, phase_pops)
```

```python
import jax
import jax.numpy as jnp
from jax import lax
from jax.experimental import pallas as pl
from jax.experimental.pallas import tpu as pltpu
from jax.sharding import PartitionSpec as P

AXES = ("gx", "gy", "gz")

VEL_F = [
    (0, 0, 0),
    (1, 0, 0),
    (-1, 0, 0),
    (0, 1, 0),
    (0, -1, 0),
    (0, 0, 1),
    (0, 0, -1),
    (1, 1, 0),
    (-1, -1, 0),
    (1, -1, 0),
    (-1, 1, 0),
    (1, 0, 1),
    (-1, 0, -1),
    (1, 0, -1),
    (-1, 0, 1),
    (0, 1, 1),
    (0, -1, -1),
    (0, 1, -1),
    (0, -1, 1),
]
OPP_F = [0, 2, 1, 4, 3, 6, 5, 8, 7, 10, 9, 12, 11, 14, 13, 16, 15, 18, 17]
NF = 19
NG = 7
NP = NF + NG
VEL = VEL_F + VEL_F[:NG]
OPP = OPP_F + [NF + other for other in OPP_F[:NG]]

HALO = 4
ROCK = 3.0e38

IN_F = [1, 7, 9, 11, 13]
IN_G = 1
L_G2 = 0
L_F2 = L_G2 + NG
L_RHO2 = L_F2 + len(IN_F)
L_MOM2 = L_RHO2 + 1
L_G3 = L_MOM2 + 3
L_PH3 = L_G3 + 1
L_UX3 = L_PH3 + 1
L_PH4 = L_UX3 + 1
L_MASK = L_PH4 + 1
L_STRIP = L_MASK + 3


def pairing(sizes, axis, first):
    spare = "gy" if axis != "gy" else "gx"
    perm = []
    real = False

    def linear(at):
        return (at["gx"] * sizes["gy"] + at["gy"]) * sizes["gz"] + at["gz"]

    for gx in range(sizes["gx"]):
        for gy in range(sizes["gy"]):
            for gz in range(sizes["gz"]):
                at = {"gx": gx, "gy": gy, "gz": gz}
                other = at[axis] + (1 if at[axis] % 2 == first else -1)
                if 0 <= other < sizes[axis]:
                    real = True
                    perm.append((linear(at), linear({**at, axis: other})))
                elif at[spare] ^ 1 < sizes[spare]:
                    perm.append((linear(at), linear({**at, spare: at[spare] ^ 1})))
    return perm if real else None


def swap(sizes, axis, send_a, send_b):
    perm_a = pairing(sizes, axis, 0)
    perm_b = pairing(sizes, axis, 1)
    got_a = lax.ppermute(send_a, AXES, perm_a) if perm_a else send_a
    got_b = lax.ppermute(send_b, AXES, perm_b) if perm_b else got_a
    return got_a, got_b


def beside(sizes, cells):
    if sizes["gy"] <= 2:
        perm = pairing(sizes, "gy", 0)
        return lax.ppermute(cells, AXES, perm) if perm else cells
    got_a, got_b = swap(sizes, "gy", cells, cells)
    even = lax.axis_index("gy") % 2 == 0
    above = jnp.where(even, got_a, got_b)
    below = jnp.where(even, got_b, got_a)
    row = lax.broadcasted_iota(jnp.int32, cells.shape, cells.ndim - 2)
    return jnp.where(row < HALO, above, below)


def relax(rho, mom, phase, grads, pops):
    inv = 1.0 / rho if rho is not None else None
    vel = [m * inv if inv is not None else m for m in mom]
    square = grads[0] * grads[0] + grads[1] * grads[1] + grads[2] * grads[2] + 0.01
    inv_mag = lax.rsqrt(square)
    mag = square * inv_mag
    out = {}
    if any(member < NF for member in pops):
        omega = 1.0 / (0.8 + 0.2 * phase)
        keep = 1.0 - omega
        scale = omega * rho
        base = scale * (1.0 - 1.5 * (vel[0] * vel[0] + vel[1] * vel[1] + vel[2] * vel[2]))
        quad_v = [4.5 * scale * v for v in vel]
        quad_g = [0.5 * inv_mag * g for g in grads]
        lin = [(3.0 * scale) * v for v in vel]
        diag = [quad_v[d] * vel[d] + quad_g[d] * grads[d] for d in range(3)]
        tail = {
            0: (1.0 / 9.0) * mag,
            1: (-0.5 / 54.0) * mag,
            2: (-0.5 / 27.0) * mag,
        }
        memo = {}

        def once(key, make):
            if key not in memo:
                memo[key] = make()
            return memo[key]

        for member in pops:
            if member >= NF:
                continue
            dims = [d for d in range(3) if VEL[member][d] != 0]
            signs = [VEL[member][d] for d in dims]
            if not dims:
                out[member] = keep * pops[member] + ((1.0 / 3.0) * base + tail[0])
                continue
            if len(dims) == 1:
                d = dims[0]
                even = once(("e", d), lambda: (1.0 / 18.0) * (base + diag[d]) + tail[1])
                odd = once(("o", d), lambda: (1.0 / 18.0) * lin[d])
                flip = signs[0]
            else:
                a, b = dims
                same = signs[0] * signs[1]
                both = once(("s", a, b), lambda: base + diag[a] + diag[b])
                mixed = once(
                    ("m", a, b),
                    lambda: 2.0 * (quad_v[a] * vel[b] + quad_g[a] * grads[b]),
                )
                even = once(
                    ("e", a, b, same),
                    lambda: (1.0 / 36.0) * (both + mixed if same > 0 else both - mixed) + tail[2],
                )
                odd = once(
                    ("o", a, b, same),
                    lambda: (1.0 / 36.0) * (lin[a] + lin[b] if same > 0 else lin[a] - lin[b]),
                )
                flip = signs[0]
            mid = keep * pops[member] + even
            out[member] = mid + odd if flip > 0 else mid - odd
    if any(member >= NF for member in pops):
        sharpen = 0.7 * (1.0 - phase * phase) * inv_mag
        part = 1.25 * 0.125
        for member in pops:
            if member < NF:
                continue
            move = VEL[member]
            if move == (0, 0, 0):
                out[member] = (1.25 * 0.25) * phase - 0.25 * pops[member]
                continue
            d = [i for i in range(3) if move[i] != 0][0]
            drift = part * (4.0 * phase * vel[d] + sharpen * grads[d])
            still = part * phase - 0.25 * pops[member]
            out[member] = still + drift if move[d] > 0 else still - drift
    return out


def moments(pops):
    rho = pops[0]
    for member in range(1, NF):
        rho = rho + pops[member]
    mom = []
    for d in range(3):
        plus = [pops[m] for m in range(NF) if VEL[m][d] > 0]
        minus = [pops[m] for m in range(NF) if VEL[m][d] < 0]
        total = plus[0] - minus[0]
        for p, m in zip(plus[1:], minus[1:]):
            total = total + (p - m)
        mom.append(total)
    return rho, mom


def add_up(values):
    total = values[0]
    for value in values[1:]:
        total = total + value
    return total


def turn(value, shift, dim):
    size = value.shape[dim]
    shift = shift % size
    return pltpu.roll(value, shift, axis=dim) if shift else value


def pack_z_kernel(flow, phase, mask, out_a, out_b):
    cx, cy, cz = mask.shape
    even = lax.axis_index("gz") % 2 == 0
    group = lax.broadcasted_iota(jnp.int32, (cy, cz), 1) // HALO
    per = cz // (cx * HALO)
    for block in range(out_a.shape[0]):
        low = jnp.zeros((cy, cz), jnp.float32)
        high = low
        for field in range(block * per, min((block + 1) * per, NP + 1)):
            for x in range(cx):
                if field < NF:
                    value = flow[field, x]
                elif field < NP:
                    value = phase[field - NF, x]
                else:
                    value = mask[x].astype(jnp.float32)
                slot = (field % per) * cx + x
                here = group == slot
                low = jnp.where(here, turn(value, slot * HALO, 1), low)
                high = jnp.where(here, turn(value, (slot + 1) * HALO, 1), high)
        out_a[block] = jnp.where(even, high, low)
        out_b[block] = jnp.where(even, low, high)


def pack_x_kernel(flow, phase, mask, z_a, z_b, strips, out_a, out_b, *, sizes):
    cx, cy, cz = mask.shape
    at_z = lax.axis_index("gz")
    even_z = at_z % 2 == 0
    even_x = lax.axis_index("gx") % 2 == 0
    group = lax.broadcasted_iota(jnp.int32, (cy, cz), 1) // HALO
    per_in = cz // (cx * HALO)
    per_out = cz // (4 * cx * HALO)
    below = [jnp.where(even_z, z_b[i], z_a[i]) for i in range(z_a.shape[0])]
    above = [jnp.where(even_z, z_a[i], z_b[i]) for i in range(z_a.shape[0])]
    has_below = at_z > 0
    has_above = at_z < sizes["gz"] - 1
    for block in range(strips.shape[0]):
        total = jnp.zeros((cy, cz), jnp.float32)
        for field in range(block * per_out, min((block + 1) * per_out, NP + 1)):
            from_below = below[field // per_in]
            from_above = above[field // per_in]
            if field == NP:
                from_below = jnp.where(has_below, from_below, 0.0)
                from_above = jnp.where(has_above, from_above, 0.0)
            for x in range(cx):
                if field < NF:
                    value = flow[field, x]
                elif field < NP:
                    value = phase[field - NF, x]
                else:
                    value = mask[x].astype(jnp.float32)
                came = (field % per_in) * cx + x
                base = (field % per_out) * 4 * cx
                for piece, origin, slot in (
                    (from_below, came, base + 2 * x),
                    (value, 0, base + 2 * x + 1),
                    (value, cz // HALO - 1, base + 2 * (cx + x)),
                    (from_above, came, base + 2 * (cx + x) + 1),
                ):
                    total = jnp.where(
                        group == slot, turn(piece, (slot - origin) * HALO, 1), total
                    )
        strips[block] = total
        out_a[NP + L_STRIP + block] = total
        out_b[NP + L_STRIP + block] = total

    for out, up in ((out_a, even_x), (out_b, jnp.logical_not(even_x))):
        other = jnp.where(up, 0, 1)
        xs = [jnp.where(up, cx - 1 - d, d) for d in range(HALO)]
        for member in range(NF):
            out[member] = flow[member, xs[0]]
        for member in range(NG):
            out[NF + member] = phase[member, xs[0]]
            out[NP + L_G2 + member] = phase[member, xs[1]]
        for slot, member in enumerate(IN_F):
            out[NP + L_F2 + slot] = flow[member + other, xs[1]]
        rho, mom = moments([flow[member, xs[1]] for member in range(NF)])
        out[NP + L_RHO2] = rho
        for d in range(3):
            out[NP + L_MOM2 + d] = mom[d]
        out[NP + L_G3] = phase[IN_G + other, xs[2]]
        out[NP + L_PH3] = add_up([phase[member, xs[2]] for member in range(NG)])
        rho, mom = moments([flow[member, xs[2]] for member in range(NF)])
        out[NP + L_UX3] = mom[0] / rho
        far = add_up([phase[member, xs[3]] for member in range(NG)])
        out[NP + L_PH4] = jnp.where(mask[xs[3]] == 1, far, 0.0)
        for d in range(3):
            out[NP + L_MASK + d] = mask[xs[d]].astype(jnp.float32)


def steps_kernel(
    flow, phase, mask, strips, x_a, x_b,
    flow_y, phase_y, mask_y, strips_y, x_a_y, x_b_y,
    flow_out, phase_out,
    pops, face, own_mask, own_strips, fluid, potential,
    strip_pops, strip_fluid, strip_phase, moved, stayed, strip_moved, strip_stayed,
    phase_pops, potential1, moved1, stayed1, sem,
    *, sizes,
):
    _, cx, cy, cz = flow_out.shape
    rows = 2 * cy
    at_x = lax.axis_index("gx")
    at_y = lax.axis_index("gy")
    even_x = at_x % 2 == 0
    side_a = jnp.where(even_x, 1, 0)
    side_b = 1 - side_a

    copies = []

    def copy(src, dst):
        one = pltpu.make_async_copy(src, dst, sem.at[len(copies)])
        one.start()
        copies.append(one)

    for at, (f, g, m, s, a, b) in (
        (0, (flow, phase, mask, strips, x_a, x_b)),
        (cy, (flow_y, phase_y, mask_y, strips_y, x_a_y, x_b_y)),
    ):
        part = pl.ds(at, cy)
        copy(f, pops.at[pl.ds(0, NF), pl.ds(1, cx), part])
        copy(g, pops.at[pl.ds(NF, NG), pl.ds(1, cx), part])
        copy(m, own_mask.at[:, part])
        copy(s, own_strips.at[:, part])
        for got, side in ((a, side_a), (b, side_b)):
            copy(got.at[pl.ds(0, NP)], pops.at[:, side * (cx + 1), part])
            copy(got.at[pl.ds(NP, face.shape[1])], face.at[side, :, part])
    for one in copies:
        one.wait()

    lane = lax.broadcasted_iota(jnp.int32, (rows, cz), 1)
    row = lax.broadcasted_iota(jnp.int32, (rows, cz), 0)
    has_left = at_x > 0
    has_right = at_x < sizes["gx"] - 1
    has_low = at_y > 0
    has_high = at_y < sizes["gy"] - 1
    high_row = jnp.where(has_high, cy + HALO, cy)
    low_row = jnp.where(has_low, cy + HALO, rows)
    row_ok = (row < high_row) | (row >= low_row)
    has = (has_left, has_right)
    first, last = HALO, HALO + cx - 1

    def at_depth(side, depth):
        return first - depth if side == 0 else last + depth

    for x in range(cx):
        ok = (own_mask[x] == 1) & row_ok
        fluid[first + x] = ok.astype(jnp.float32)
        total = add_up([pops[NF + member, 1 + x] for member in range(NG)])
        potential[first + x] = jnp.where(ok, total, 0.0)
    for side in range(2):
        side_ok = row_ok & has[side]
        for depth in range(1, HALO + 1):
            if depth == 1:
                total = add_up([pops[NF + m, side * (cx + 1)] for m in range(NG)])
            elif depth == 2:
                total = add_up([face[side, L_G2 + m] for m in range(NG)])
            else:
                total = face[side, L_PH3 if depth == 3 else L_PH4]
            ok = side_ok
            if depth < HALO:
                ok = ok & (face[side, L_MASK + depth - 1] == 1.0)
                fluid[at_depth(side, depth)] = ok.astype(jnp.float32)
            potential[at_depth(side, depth)] = jnp.where(ok, total, 0.0)

    cols = 2 * HALO
    wide = cols * cx
    per = cz // (2 * wide)
    block_ok = row_ok & (
        ((lane < wide) & has_left)
        | ((lane >= wide) & (lane < 2 * wide))
        | ((lane >= 2 * wide) & (lane < 3 * wide) & has_right)
    )
    for side in range(2):
        for field in range(NP + 1):
            block = field // per
            origin = ((field % per) * 2 + side) * wide
            left = turn(face[0, L_STRIP + block], -origin, 1)
            mine = turn(own_strips[block], wide - origin, 1)
            right = turn(face[1, L_STRIP + block], 2 * wide - origin, 1)
            value = jnp.where(lane < wide, left, jnp.where(lane < 2 * wide, mine, right))
            if field < NP:
                strip_pops[side, field] = value
            else:
                strip_fluid[side] = jnp.where(block_ok, value, 0.0)

    def strip_grads(values):
        return (
            0.5 * (turn(values, -cols, 1) - turn(values, cols, 1)),
            0.5 * (turn(values, -1, 0) - turn(values, 1, 0)),
            0.5 * (turn(values, -1, 1) - turn(values, 1, 1)),
        )

    def push_strip(member, value, ok):
        move = VEL[member]
        value = jnp.where(ok, value, ROCK)
        value = turn(value, move[0] * cols + move[2], 1)
        return turn(value, move[1], 0)

    def strip_to_lane(side, values, at):
        if side == 0:
            return pltpu.roll(values, (2 * cz - (at * cols + HALO)) % cz, axis=1)
        return pltpu.roll(values, (cz - HALO - at * cols) % cz, axis=1)

    def main_grads(source, strip_source, at):
        here = source[at]
        down = jnp.where(lane == 0, strip_to_lane(0, strip_source[0], at), turn(here, 1, 1))
        up = jnp.where(
            lane == cz - 1, strip_to_lane(1, strip_source[1], at), turn(here, -1, 1)
        )
        return (
            0.5 * (source[at + 1] - source[at - 1]),
            0.5 * (turn(here, -1, 0) - turn(here, 1, 0)),
            0.5 * (up - down),
        )

    def push_main(member, value, ok, strip_source, at):
        move = VEL[member]
        value = jnp.where(ok, value, ROCK)
        value = turn(value, move[1], 0)
        if move[2] > 0:
            value = jnp.where(
                lane == 0, strip_to_lane(0, strip_source[0, member], at + move[0]), turn(value, 1, 1)
            )
        elif move[2] < 0:
            value = jnp.where(
                lane == cz - 1,
                strip_to_lane(1, strip_source[1, member], at + move[0]),
                turn(value, -1, 1),
            )
        return value

    for side in range(2):
        ok = strip_fluid[side] == 1.0
        values = [strip_pops[side, member] for member in range(NP)]
        total = jnp.where(ok, add_up(values[NF:]), 0.0)
        strip_phase[side] = turn(total, 1 if side == 0 else -1, 1)
        rho, mom = moments(values)
        done = relax(rho, mom, total, strip_grads(total), dict(enumerate(values)))
        for member in range(NP):
            strip_stayed[side, member] = done[member]
            strip_moved[side, member] = push_strip(member, done[member], ok)

    def collide(j, carry):
        at = first - 1 + j
        values = [pops[member, j] for member in range(NP)]
        ok = fluid[at] == 1.0
        rho, mom = moments(values)
        done = relax(
            rho, mom, potential[at], main_grads(potential, strip_phase, at),
            dict(enumerate(values)),
        )
        for member in range(NP):
            stayed[member, at] = done[member]
            moved[member, at] = push_main(member, done[member], ok, strip_moved, at)
        return carry

    lax.fori_loop(0, cx + 2, collide, 0)
    for side in range(2):
        at = at_depth(side, 2)
        members = {m + side: face[side, L_F2 + slot] for slot, m in enumerate(IN_F)}
        members.update({NF + m: face[side, L_G2 + m] for m in range(NG)})
        done = relax(
            face[side, L_RHO2], [face[side, L_MOM2 + d] for d in range(3)],
            potential[at], main_grads(potential, strip_phase, at), members,
        )
        ok = fluid[at] == 1.0
        for member in done:
            stayed[member, at] = done[member]
            moved[member, at] = push_main(member, done[member], ok, strip_moved, at)
        at = at_depth(side, 3)
        member = NF + IN_G + side
        done = relax(
            None, [face[side, L_UX3]] * 3, potential[at],
            main_grads(potential, strip_phase, at), {member: face[side, L_G3]},
        )
        ok = fluid[at] == 1.0
        moved[member, at] = push_main(member, done[member], ok, strip_moved, at)

    def pull(source, kept, member, at):
        if VEL[member] == (0, 0, 0):
            return kept[member, at]
        value = source[member, at - VEL[member][0]]
        return jnp.where(value == ROCK, kept[OPP[member], at], value)

    def stream(j, carry):
        at = first - 2 + j
        values = [pull(moved, stayed, NF + member, at) for member in range(NG)]
        for member in range(NG):
            phase_pops[member, at] = values[member]
        potential1[at] = jnp.where(fluid[at] == 1.0, add_up(values), 0.0)
        return carry

    lax.fori_loop(0, cx + 4, stream, 0)

    for side in range(2):
        ok = strip_fluid[side] == 1.0
        values = []
        for member in range(NP):
            value = strip_moved[side, member]
            back = strip_stayed[side, OPP[member]]
            values.append(jnp.where(value == ROCK, back, value))
        total = jnp.where(ok, add_up(values[NF:]), 0.0)
        rho, mom = moments(values)
        sign = 1 if side == 0 else -1
        wanted = {m: values[m] for m in range(NP) if VEL[m][2] == sign}
        done = relax(rho, mom, total, strip_grads(total), wanted)
        for member in wanted:
            strip_pops[side, member] = push_strip(member, done[member], ok)
        strip_phase[side] = turn(total, sign, 1)

    def collide1(j, carry):
        at = first - 1 + j
        values = [pull(moved, stayed, member, at) for member in range(NF)]
        values += [phase_pops[member, at] for member in range(NG)]
        ok = fluid[at] == 1.0
        rho, mom = moments(values)
        done = relax(
            rho, mom, potential1[at], main_grads(potential1, strip_phase, at),
            dict(enumerate(values)),
        )
        for member in range(NP):
            stayed1[member, at] = done[member]
            moved1[member, at] = push_main(member, done[member], ok, strip_pops, at)
        return carry

    lax.fori_loop(0, cx + 2, collide1, 0)

    def finish(x, carry):
        at = first + x
        own = pl.ds(0, cy)
        ok = fluid[at, own] == 1.0
        for member in range(NP):
            if VEL[member] == (0, 0, 0):
                value = stayed1[member, at, own]
            else:
                value = moved1[member, at - VEL[member][0], own]
                value = jnp.where(value == ROCK, stayed1[OPP[member], at, own], value)
            value = jnp.where(ok, value, pops[member, 1 + x, own])
            if member < NF:
                flow_out[member, x] = value
            else:
                phase_out[member - NF, x] = value
        return carry

    lax.fori_loop(0, cx, finish, 0)


def shards(sizes, flow_pops, phase_pops, pore_mask):
    cx, cy, cz = pore_mask.shape
    rows = 2 * cy
    assert cx >= HALO and cy == 2 * HALO and 6 * cx * HALO <= cz
    f32 = jnp.float32
    vmem = pl.BlockSpec(memory_space=pltpu.VMEM)
    anywhere = pl.BlockSpec(memory_space=pl.ANY)

    flow_y = beside(sizes, flow_pops)
    phase_y = beside(sizes, phase_pops)
    mask_y = beside(sizes, pore_mask)

    z_blocks = pl.cdiv(NP + 1, cz // (cx * HALO))
    z_shape = jax.ShapeDtypeStruct((z_blocks, cy, cz), f32)
    z_a, z_b = pl.pallas_call(
        pack_z_kernel,
        out_shape=(z_shape, z_shape),
        in_specs=[vmem] * 3,
        out_specs=(vmem, vmem),
        name="pack_z",
    )(flow_pops, phase_pops, pore_mask)
    z_a, z_b = swap(sizes, "gz", z_a, z_b)

    strip_blocks = pl.cdiv(NP + 1, cz // (4 * cx * HALO))
    strip_shape = jax.ShapeDtypeStruct((strip_blocks, cy, cz), f32)
    x_layers = NP + L_STRIP + strip_blocks
    x_shape = jax.ShapeDtypeStruct((x_layers, cy, cz), f32)
    strips, x_a, x_b = pl.pallas_call(
        lambda *refs: pack_x_kernel(*refs, sizes=sizes),
        out_shape=(strip_shape, x_shape, x_shape),
        in_specs=[vmem] * 5,
        out_specs=(vmem,) * 3,
        name="pack_x",
    )(flow_pops, phase_pops, pore_mask, z_a, z_b)
    strips_y = beside(sizes, strips)
    x_a, x_b = swap(sizes, "gx", x_a, x_b)
    x_a_y = beside(sizes, x_a)
    x_b_y = beside(sizes, x_b)

    deep = cx + 2 * HALO

    def block(*lead):
        return pltpu.VMEM((*lead, rows, cz), f32)

    return pl.pallas_call(
        lambda *refs: steps_kernel(*refs, sizes=sizes),
        out_shape=(
            jax.ShapeDtypeStruct(flow_pops.shape, f32),
            jax.ShapeDtypeStruct(phase_pops.shape, f32),
        ),
        in_specs=[anywhere] * 12,
        out_specs=(vmem, vmem),
        scratch_shapes=[
            block(NP, cx + 2),
            block(2, L_STRIP + strip_blocks),
            pltpu.VMEM((cx, rows, cz), jnp.int32),
            block(strip_blocks),
            block(deep),
            block(deep),
            block(2, NP),
            block(2),
            block(2),
            block(NP, deep),
            block(NP, deep),
            block(2, NP),
            block(2, NP),
            block(NG, deep),
            block(deep),
            block(NP, deep),
            block(NP, deep),
            pltpu.SemaphoreType.DMA((16,)),
        ],
        name="two_steps",
    )(
        flow_pops, phase_pops, pore_mask, strips, x_a, x_b,
        flow_y, phase_y, mask_y, strips_y, x_a_y, x_b_y,
    )


def solution(mesh):
    sizes = dict(mesh.shape)
    placed = (P(None, "gx", "gy", "gz"), P(None, "gx", "gy", "gz"), P("gx", "gy", "gz"))
    return jax.shard_map(
        lambda *args: shards(sizes, *args),
        mesh=mesh,
        in_specs=placed,
        out_specs=(P(None, "gx", "gy", "gz"), P(None, "gx", "gy", "gz")),
        check_vma=False,
    )
```

```python
import jax
import jax.numpy as jnp
from jax import lax
from jax.experimental import pallas as pl
from jax.experimental.pallas import tpu as pltpu
from jax.sharding import PartitionSpec as P

AXES = ("gx", "gy", "gz")

VEL_F = [
    (0, 0, 0),
    (1, 0, 0),
    (-1, 0, 0),
    (0, 1, 0),
    (0, -1, 0),
    (0, 0, 1),
    (0, 0, -1),
    (1, 1, 0),
    (-1, -1, 0),
    (1, -1, 0),
    (-1, 1, 0),
    (1, 0, 1),
    (-1, 0, -1),
    (1, 0, -1),
    (-1, 0, 1),
    (0, 1, 1),
    (0, -1, -1),
    (0, 1, -1),
    (0, -1, 1),
]
OPP_F = [0, 2, 1, 4, 3, 6, 5, 8, 7, 10, 9, 12, 11, 14, 13, 16, 15, 18, 17]
NF = 19
NG = 7
NP = NF + NG
VEL = VEL_F + VEL_F[:NG]
OPP = OPP_F + [NF + other for other in OPP_F[:NG]]

HALO = 4
ROCK = 3.0e38

IN_F = [1, 7, 9, 11, 13]
IN_G = 1
L_G2 = 0
L_F2 = L_G2 + NG
L_RHO2 = L_F2 + len(IN_F)
L_MOM2 = L_RHO2 + 1
L_G3 = L_MOM2 + 3
L_PH3 = L_G3 + 1
L_UX3 = L_PH3 + 1
L_PH4 = L_UX3 + 1
L_MASK = L_PH4 + 1
L_STRIP = L_MASK + 3


def pairing(sizes, axis, first):
    spare = "gy" if axis != "gy" else "gx"
    perm = []
    real = False

    def linear(at):
        return (at["gx"] * sizes["gy"] + at["gy"]) * sizes["gz"] + at["gz"]

    for gx in range(sizes["gx"]):
        for gy in range(sizes["gy"]):
            for gz in range(sizes["gz"]):
                at = {"gx": gx, "gy": gy, "gz": gz}
                other = at[axis] + (1 if at[axis] % 2 == first else -1)
                if 0 <= other < sizes[axis]:
                    real = True
                    perm.append((linear(at), linear({**at, axis: other})))
                elif at[spare] ^ 1 < sizes[spare]:
                    perm.append((linear(at), linear({**at, spare: at[spare] ^ 1})))
    return perm if real else None


def swap(sizes, axis, send_a, send_b):
    perm_a = pairing(sizes, axis, 0)
    perm_b = pairing(sizes, axis, 1)
    got_a = lax.ppermute(send_a, AXES, perm_a) if perm_a else send_a
    got_b = lax.ppermute(send_b, AXES, perm_b) if perm_b else got_a
    return got_a, got_b


def beside(sizes, cells):
    if sizes["gy"] <= 2:
        perm = pairing(sizes, "gy", 0)
        return lax.ppermute(cells, AXES, perm) if perm else cells
    got_a, got_b = swap(sizes, "gy", cells, cells)
    even = lax.axis_index("gy") % 2 == 0
    above = jnp.where(even, got_a, got_b)
    below = jnp.where(even, got_b, got_a)
    row = lax.broadcasted_iota(jnp.int32, cells.shape, cells.ndim - 2)
    return jnp.where(row < HALO, above, below)


def relax(rho, mom, phase, grads, pops):
    inv = 1.0 / rho if rho is not None else None
    vel = [m * inv if inv is not None else m for m in mom]
    square = grads[0] * grads[0] + grads[1] * grads[1] + grads[2] * grads[2] + 0.01
    inv_mag = lax.rsqrt(square)
    mag = square * inv_mag
    out = {}
    if any(member < NF for member in pops):
        omega = 1.0 / (0.8 + 0.2 * phase)
        keep = 1.0 - omega
        scale = omega * rho
        base = scale * (1.0 - 1.5 * (vel[0] * vel[0] + vel[1] * vel[1] + vel[2] * vel[2]))
        quad_v = [4.5 * scale * v for v in vel]
        quad_g = [0.5 * inv_mag * g for g in grads]
        lin = [(3.0 * scale) * v for v in vel]
        diag = [quad_v[d] * vel[d] + quad_g[d] * grads[d] for d in range(3)]
        tail = {
            0: (1.0 / 9.0) * mag,
            1: (-0.5 / 54.0) * mag,
            2: (-0.5 / 27.0) * mag,
        }
        memo = {}

        def once(key, make):
            if key not in memo:
                memo[key] = make()
            return memo[key]

        for member in pops:
            if member >= NF:
                continue
            dims = [d for d in range(3) if VEL[member][d] != 0]
            signs = [VEL[member][d] for d in dims]
            if not dims:
                out[member] = keep * pops[member] + ((1.0 / 3.0) * base + tail[0])
                continue
            if len(dims) == 1:
                d = dims[0]
                even = once(("e", d), lambda: (1.0 / 18.0) * (base + diag[d]) + tail[1])
                odd = once(("o", d), lambda: (1.0 / 18.0) * lin[d])
                flip = signs[0]
            else:
                a, b = dims
                same = signs[0] * signs[1]
                both = once(("s", a, b), lambda: base + diag[a] + diag[b])
                mixed = once(
                    ("m", a, b),
                    lambda: 2.0 * (quad_v[a] * vel[b] + quad_g[a] * grads[b]),
                )
                even = once(
                    ("e", a, b, same),
                    lambda: (1.0 / 36.0) * (both + mixed if same > 0 else both - mixed) + tail[2],
                )
                odd = once(
                    ("o", a, b, same),
                    lambda: (1.0 / 36.0) * (lin[a] + lin[b] if same > 0 else lin[a] - lin[b]),
                )
                flip = signs[0]
            mid = keep * pops[member] + even
            out[member] = mid + odd if flip > 0 else mid - odd
    if any(member >= NF for member in pops):
        sharpen = 0.7 * (1.0 - phase * phase) * inv_mag
        part = 1.25 * 0.125
        for member in pops:
            if member < NF:
                continue
            move = VEL[member]
            if move == (0, 0, 0):
                out[member] = (1.25 * 0.25) * phase - 0.25 * pops[member]
                continue
            d = [i for i in range(3) if move[i] != 0][0]
            drift = part * (4.0 * phase * vel[d] + sharpen * grads[d])
            still = part * phase - 0.25 * pops[member]
            out[member] = still + drift if move[d] > 0 else still - drift
    return out


def moments(pops):
    rho = pops[0]
    for member in range(1, NF):
        rho = rho + pops[member]
    mom = []
    for d in range(3):
        plus = [pops[m] for m in range(NF) if VEL[m][d] > 0]
        minus = [pops[m] for m in range(NF) if VEL[m][d] < 0]
        total = plus[0] - minus[0]
        for p, m in zip(plus[1:], minus[1:]):
            total = total + (p - m)
        mom.append(total)
    return rho, mom


def add_up(values):
    total = values[0]
    for value in values[1:]:
        total = total + value
    return total


def turn(value, shift, dim):
    size = value.shape[dim]
    shift = shift % size
    return pltpu.roll(value, shift, axis=dim) if shift else value


def pack_z_kernel(flow, phase, mask, out_a, out_b):
    cx, cy, cz = mask.shape
    even = lax.axis_index("gz") % 2 == 0
    group = lax.broadcasted_iota(jnp.int32, (cy, cz), 1) // HALO
    per = cz // (cx * HALO)
    for block in range(out_a.shape[0]):
        low = jnp.zeros((cy, cz), jnp.float32)
        high = low
        for field in range(block * per, min((block + 1) * per, NP + 1)):
            for x in range(cx):
                if field < NF:
                    value = flow[field, x]
                elif field < NP:
                    value = phase[field - NF, x]
                else:
                    value = mask[x].astype(jnp.float32)
                slot = (field % per) * cx + x
                here = group == slot
                low = jnp.where(here, turn(value, slot * HALO, 1), low)
                high = jnp.where(here, turn(value, (slot + 1) * HALO, 1), high)
        out_a[block] = jnp.where(even, high, low)
        out_b[block] = jnp.where(even, low, high)


def pack_x_kernel(flow, phase, mask, z_a, z_b, strips, out_a, out_b, *, sizes):
    cx, cy, cz = mask.shape
    at_z = lax.axis_index("gz")
    even_z = at_z % 2 == 0
    even_x = lax.axis_index("gx") % 2 == 0
    group = lax.broadcasted_iota(jnp.int32, (cy, cz), 1) // HALO
    per_in = cz // (cx * HALO)
    per_out = cz // (4 * cx * HALO)
    below = [jnp.where(even_z, z_b[i], z_a[i]) for i in range(z_a.shape[0])]
    above = [jnp.where(even_z, z_a[i], z_b[i]) for i in range(z_a.shape[0])]
    has_below = at_z > 0
    has_above = at_z < sizes["gz"] - 1
    for block in range(strips.shape[0]):
        total = jnp.zeros((cy, cz), jnp.float32)
        for field in range(block * per_out, min((block + 1) * per_out, NP + 1)):
            from_below = below[field // per_in]
            from_above = above[field // per_in]
            if field == NP:
                from_below = jnp.where(has_below, from_below, 0.0)
                from_above = jnp.where(has_above, from_above, 0.0)
            for x in range(cx):
                if field < NF:
                    value = flow[field, x]
                elif field < NP:
                    value = phase[field - NF, x]
                else:
                    value = mask[x].astype(jnp.float32)
                came = (field % per_in) * cx + x
                base = (field % per_out) * 4 * cx
                for piece, origin, slot in (
                    (from_below, came, base + 2 * x),
                    (value, 0, base + 2 * x + 1),
                    (value, cz // HALO - 1, base + 2 * (cx + x)),
                    (from_above, came, base + 2 * (cx + x) + 1),
                ):
                    total = jnp.where(
                        group == slot, turn(piece, (slot - origin) * HALO, 1), total
                    )
        strips[block] = total
        out_a[NP + L_STRIP + block] = total
        out_b[NP + L_STRIP + block] = total

    for out, up in ((out_a, even_x), (out_b, jnp.logical_not(even_x))):
        other = jnp.where(up, 0, 1)
        xs = [jnp.where(up, cx - 1 - d, d) for d in range(HALO)]
        for member in range(NF):
            out[member] = flow[member, xs[0]]
        for member in range(NG):
            out[NF + member] = phase[member, xs[0]]
            out[NP + L_G2 + member] = phase[member, xs[1]]
        for slot, member in enumerate(IN_F):
            out[NP + L_F2 + slot] = flow[member + other, xs[1]]
        rho, mom = moments([flow[member, xs[1]] for member in range(NF)])
        out[NP + L_RHO2] = rho
        for d in range(3):
            out[NP + L_MOM2 + d] = mom[d]
        out[NP + L_G3] = phase[IN_G + other, xs[2]]
        out[NP + L_PH3] = add_up([phase[member, xs[2]] for member in range(NG)])
        rho, mom = moments([flow[member, xs[2]] for member in range(NF)])
        out[NP + L_UX3] = mom[0] / rho
        far = add_up([phase[member, xs[3]] for member in range(NG)])
        out[NP + L_PH4] = jnp.where(mask[xs[3]] == 1, far, 0.0)
        for d in range(3):
            out[NP + L_MASK + d] = mask[xs[d]].astype(jnp.float32)


def steps_kernel(
    flow, phase, mask, strips, x_a, x_b,
    flow_y, phase_y, mask_y, strips_y, x_a_y, x_b_y,
    flow_out, phase_out,
    pops, face, own_mask, own_strips, fluid, potential,
    strip_pops, strip_fluid, strip_phase, moved, stayed, strip_moved, strip_stayed,
    phase_pops, potential1, moved1, stayed1, sem,
    *, sizes,
):
    _, cx, cy, cz = flow_out.shape
    rows = 2 * cy
    at_x = lax.axis_index("gx")
    at_y = lax.axis_index("gy")
    even_x = at_x % 2 == 0
    side_a = jnp.where(even_x, 1, 0)
    side_b = 1 - side_a

    copies = []

    def copy(src, dst):
        one = pltpu.make_async_copy(src, dst, sem.at[len(copies)])
        one.start()
        copies.append(one)

    for at, (f, g, m, s, a, b) in (
        (0, (flow, phase, mask, strips, x_a, x_b)),
        (cy, (flow_y, phase_y, mask_y, strips_y, x_a_y, x_b_y)),
    ):
        part = pl.ds(at, cy)
        copy(f, pops.at[pl.ds(0, NF), pl.ds(1, cx), part])
        copy(g, pops.at[pl.ds(NF, NG), pl.ds(1, cx), part])
        copy(m, own_mask.at[:, part])
        copy(s, own_strips.at[:, part])
        for got, side in ((a, side_a), (b, side_b)):
            copy(got.at[pl.ds(0, NP)], pops.at[:, side * (cx + 1), part])
            copy(got.at[pl.ds(NP, face.shape[1])], face.at[side, :, part])
    for one in copies:
        one.wait()

    lane = lax.broadcasted_iota(jnp.int32, (rows, cz), 1)
    row = lax.broadcasted_iota(jnp.int32, (rows, cz), 0)
    has_left = at_x > 0
    has_right = at_x < sizes["gx"] - 1
    has_low = at_y > 0
    has_high = at_y < sizes["gy"] - 1
    high_row = jnp.where(has_high, cy + HALO, cy)
    low_row = jnp.where(has_low, cy + HALO, rows)
    row_ok = (row < high_row) | (row >= low_row)
    has = (has_left, has_right)
    first, last = HALO, HALO + cx - 1

    def at_depth(side, depth):
        return first - depth if side == 0 else last + depth

    for x in range(cx):
        ok = (own_mask[x] == 1) & row_ok
        fluid[first + x] = ok.astype(jnp.float32)
        total = add_up([pops[NF + member, 1 + x] for member in range(NG)])
        potential[first + x] = jnp.where(ok, total, 0.0)
    for side in range(2):
        side_ok = row_ok & has[side]
        for depth in range(1, HALO + 1):
            if depth == 1:
                total = add_up([pops[NF + m, side * (cx + 1)] for m in range(NG)])
            elif depth == 2:
                total = add_up([face[side, L_G2 + m] for m in range(NG)])
            else:
                total = face[side, L_PH3 if depth == 3 else L_PH4]
            ok = side_ok
            if depth < HALO:
                ok = ok & (face[side, L_MASK + depth - 1] == 1.0)
                fluid[at_depth(side, depth)] = ok.astype(jnp.float32)
            potential[at_depth(side, depth)] = jnp.where(ok, total, 0.0)

    cols = 2 * HALO
    wide = cols * cx
    per = cz // (2 * wide)
    block_ok = row_ok & (
        ((lane < wide) & has_left)
        | ((lane >= wide) & (lane < 2 * wide))
        | ((lane >= 2 * wide) & (lane < 3 * wide) & has_right)
    )
    for side in range(2):
        for field in range(NP + 1):
            block = field // per
            origin = ((field % per) * 2 + side) * wide
            left = turn(face[0, L_STRIP + block], -origin, 1)
            mine = turn(own_strips[block], wide - origin, 1)
            right = turn(face[1, L_STRIP + block], 2 * wide - origin, 1)
            value = jnp.where(lane < wide, left, jnp.where(lane < 2 * wide, mine, right))
            if field < NP:
                strip_pops[side, field] = value
            else:
                strip_fluid[side] = jnp.where(block_ok, value, 0.0)

    def strip_grads(values):
        return (
            0.5 * (turn(values, -cols, 1) - turn(values, cols, 1)),
            0.5 * (turn(values, -1, 0) - turn(values, 1, 0)),
            0.5 * (turn(values, -1, 1) - turn(values, 1, 1)),
        )

    def push_strip(member, value, ok):
        move = VEL[member]
        value = jnp.where(ok, value, ROCK)
        value = turn(value, move[0] * cols + move[2], 1)
        return turn(value, move[1], 0)

    def strip_to_lane(side, values, at):
        if side == 0:
            return pltpu.roll(values, (2 * cz - (at * cols + HALO)) % cz, axis=1)
        return pltpu.roll(values, (cz - HALO - at * cols) % cz, axis=1)

    def main_grads(source, strip_source, at):
        here = source[at]
        down = jnp.where(lane == 0, strip_to_lane(0, strip_source[0], at), turn(here, 1, 1))
        up = jnp.where(
            lane == cz - 1, strip_to_lane(1, strip_source[1], at), turn(here, -1, 1)
        )
        return (
            0.5 * (source[at + 1] - source[at - 1]),
            0.5 * (turn(here, -1, 0) - turn(here, 1, 0)),
            0.5 * (up - down),
        )

    def push_main(member, value, ok, strip_source, at):
        move = VEL[member]
        value = jnp.where(ok, value, ROCK)
        value = turn(value, move[1], 0)
        if move[2] > 0:
            value = jnp.where(
                lane == 0, strip_to_lane(0, strip_source[0, member], at + move[0]), turn(value, 1, 1)
            )
        elif move[2] < 0:
            value = jnp.where(
                lane == cz - 1,
                strip_to_lane(1, strip_source[1, member], at + move[0]),
                turn(value, -1, 1),
            )
        return value

    for side in range(2):
        ok = strip_fluid[side] == 1.0
        values = [strip_pops[side, member] for member in range(NP)]
        total = jnp.where(ok, add_up(values[NF:]), 0.0)
        strip_phase[side] = turn(total, 1 if side == 0 else -1, 1)
        rho, mom = moments(values)
        done = relax(rho, mom, total, strip_grads(total), dict(enumerate(values)))
        for member in range(NP):
            strip_stayed[side, member] = done[member]
            strip_moved[side, member] = push_strip(member, done[member], ok)

    def collide(j, carry):
        at = first - 1 + j
        values = [pops[member, j] for member in range(NP)]
        ok = fluid[at] == 1.0
        rho, mom = moments(values)
        done = relax(
            rho, mom, potential[at], main_grads(potential, strip_phase, at),
            dict(enumerate(values)),
        )
        for member in range(NP):
            stayed[member, at] = done[member]
            moved[member, at] = push_main(member, done[member], ok, strip_moved, at)
        return carry

    lax.fori_loop(0, cx + 2, collide, 0)
    for side in range(2):
        at = at_depth(side, 2)
        members = {m + side: face[side, L_F2 + slot] for slot, m in enumerate(IN_F)}
        members.update({NF + m: face[side, L_G2 + m] for m in range(NG)})
        done = relax(
            face[side, L_RHO2], [face[side, L_MOM2 + d] for d in range(3)],
            potential[at], main_grads(potential, strip_phase, at), members,
        )
        ok = fluid[at] == 1.0
        for member in done:
            stayed[member, at] = done[member]
            moved[member, at] = push_main(member, done[member], ok, strip_moved, at)
        at = at_depth(side, 3)
        member = NF + IN_G + side
        done = relax(
            None, [face[side, L_UX3]] * 3, potential[at],
            main_grads(potential, strip_phase, at), {member: face[side, L_G3]},
        )
        ok = fluid[at] == 1.0
        moved[member, at] = push_main(member, done[member], ok, strip_moved, at)

    def pull(source, kept, member, at):
        if VEL[member] == (0, 0, 0):
            return kept[member, at]
        value = source[member, at - VEL[member][0]]
        return jnp.where(value == ROCK, kept[OPP[member], at], value)

    def stream(j, carry):
        at = first - 2 + j
        values = [pull(moved, stayed, NF + member, at) for member in range(NG)]
        for member in range(NG):
            phase_pops[member, at] = values[member]
        potential1[at] = jnp.where(fluid[at] == 1.0, add_up(values), 0.0)
        return carry

    lax.fori_loop(0, cx + 4, stream, 0)

    for side in range(2):
        ok = strip_fluid[side] == 1.0
        values = []
        for member in range(NP):
            value = strip_moved[side, member]
            back = strip_stayed[side, OPP[member]]
            values.append(jnp.where(value == ROCK, back, value))
        total = jnp.where(ok, add_up(values[NF:]), 0.0)
        rho, mom = moments(values)
        sign = 1 if side == 0 else -1
        wanted = {m: values[m] for m in range(NP) if VEL[m][2] == sign}
        done = relax(rho, mom, total, strip_grads(total), wanted)
        for member in wanted:
            strip_pops[side, member] = push_strip(member, done[member], ok)
        strip_phase[side] = turn(total, sign, 1)

    def collide1(j, carry):
        at = first - 1 + j
        values = [pull(moved, stayed, member, at) for member in range(NF)]
        values += [phase_pops[member, at] for member in range(NG)]
        ok = fluid[at] == 1.0
        rho, mom = moments(values)
        done = relax(
            rho, mom, potential1[at], main_grads(potential1, strip_phase, at),
            dict(enumerate(values)),
        )
        for member in range(NP):
            stayed1[member, at] = done[member]
            moved1[member, at] = push_main(member, done[member], ok, strip_pops, at)
        return carry

    lax.fori_loop(0, cx + 2, collide1, 0)

    def finish(x, carry):
        at = first + x
        own = pl.ds(0, cy)
        ok = fluid[at, own] == 1.0
        for member in range(NP):
            if VEL[member] == (0, 0, 0):
                value = stayed1[member, at, own]
            else:
                value = moved1[member, at - VEL[member][0], own]
                value = jnp.where(value == ROCK, stayed1[OPP[member], at, own], value)
            value = jnp.where(ok, value, pops[member, 1 + x, own])
            if member < NF:
                flow_out[member, x] = value
            else:
                phase_out[member - NF, x] = value
        return carry

    lax.fori_loop(0, cx, finish, 0)


def shards(sizes, flow_pops, phase_pops, pore_mask):
    cx, cy, cz = pore_mask.shape
    rows = 2 * cy
    assert cx >= HALO and cy == 2 * HALO and 6 * cx * HALO <= cz
    f32 = jnp.float32
    vmem = pl.BlockSpec(memory_space=pltpu.VMEM)
    anywhere = pl.BlockSpec(memory_space=pl.ANY)

    def near(*arrays):
        return [pltpu.with_memory_space_constraint(a, pltpu.VMEM) for a in arrays]

    flow_y = beside(sizes, flow_pops)
    phase_y = beside(sizes, phase_pops)
    mask_y = beside(sizes, pore_mask)

    z_blocks = pl.cdiv(NP + 1, cz // (cx * HALO))
    z_shape = pltpu.VMEM((z_blocks, cy, cz), f32)
    z_a, z_b = pl.pallas_call(
        pack_z_kernel,
        out_shape=(z_shape, z_shape),
        in_specs=[vmem] * 3,
        out_specs=(vmem, vmem),
        name="pack_z",
    )(*near(flow_pops, phase_pops, pore_mask))
    z_a, z_b = swap(sizes, "gz", z_a, z_b)

    strip_blocks = pl.cdiv(NP + 1, cz // (4 * cx * HALO))
    strip_shape = pltpu.VMEM((strip_blocks, cy, cz), f32)
    x_layers = NP + L_STRIP + strip_blocks
    x_shape = pltpu.VMEM((x_layers, cy, cz), f32)
    strips, x_a, x_b = pl.pallas_call(
        lambda *refs: pack_x_kernel(*refs, sizes=sizes),
        out_shape=(strip_shape, x_shape, x_shape),
        in_specs=[vmem] * 5,
        out_specs=(vmem,) * 3,
        name="pack_x",
    )(*near(flow_pops, phase_pops, pore_mask, z_a, z_b))
    strips_y = beside(sizes, strips)
    x_a, x_b = swap(sizes, "gx", x_a, x_b)
    x_a_y = beside(sizes, x_a)
    x_b_y = beside(sizes, x_b)

    deep = cx + 2 * HALO

    def block(*lead):
        return pltpu.VMEM((*lead, rows, cz), f32)

    return pl.pallas_call(
        lambda *refs: steps_kernel(*refs, sizes=sizes),
        out_shape=(
            jax.ShapeDtypeStruct(flow_pops.shape, f32),
            jax.ShapeDtypeStruct(phase_pops.shape, f32),
        ),
        in_specs=[anywhere] * 12,
        out_specs=(vmem, vmem),
        scratch_shapes=[
            block(NP, cx + 2),
            block(2, L_STRIP + strip_blocks),
            pltpu.VMEM((cx, rows, cz), jnp.int32),
            block(strip_blocks),
            block(deep),
            block(deep),
            block(2, NP),
            block(2),
            block(2),
            block(NP, deep),
            block(NP, deep),
            block(2, NP),
            block(2, NP),
            block(NG, deep),
            block(deep),
            block(NP, deep),
            block(NP, deep),
            pltpu.SemaphoreType.DMA((16,)),
        ],
        name="two_steps",
    )(
        *near(
            flow_pops, phase_pops, pore_mask, strips, x_a, x_b,
            flow_y, phase_y, mask_y, strips_y, x_a_y, x_b_y,
        )
    )


def solution(mesh):
    sizes = dict(mesh.shape)
    placed = (P(None, "gx", "gy", "gz"), P(None, "gx", "gy", "gz"), P("gx", "gy", "gz"))
    return jax.shard_map(
        lambda *args: shards(sizes, *args),
        mesh=mesh,
        in_specs=placed,
        out_specs=(P(None, "gx", "gy", "gz"), P(None, "gx", "gy", "gz")),
        check_vma=False,
    )
```

```python
import jax
import jax.numpy as jnp
from jax import lax
from jax.experimental import pallas as pl
from jax.experimental.pallas import tpu as pltpu
from jax.sharding import PartitionSpec as P


AXES = ("gx", "gy", "gz")

VEL_F = [
    (0, 0, 0),
    (1, 0, 0),
    (-1, 0, 0),
    (0, 1, 0),
    (0, -1, 0),
    (0, 0, 1),
    (0, 0, -1),
    (1, 1, 0),
    (-1, -1, 0),
    (1, -1, 0),
    (-1, 1, 0),
    (1, 0, 1),
    (-1, 0, -1),
    (1, 0, -1),
    (-1, 0, 1),
    (0, 1, 1),
    (0, -1, -1),
    (0, 1, -1),
    (0, -1, 1),
]
OPP_F = [0, 2, 1, 4, 3, 6, 5, 8, 7, 10, 9, 12, 11, 14, 13, 16, 15, 18, 17]
NF = 19
NG = 7
NP = NF + NG
VEL = VEL_F + VEL_F[:NG]
OPP = OPP_F + [NF + other for other in OPP_F[:NG]]

HALO = 4
ROCK = 3.0e38

IN_F = [1, 7, 9, 11, 13]
IN_G = 1
NV = NP + 1
L_G2 = 0
L_F2 = L_G2 + NG
L_RHO2 = L_F2 + len(IN_F)
L_MOM2 = L_RHO2 + 1
L_G3 = L_MOM2 + 3
L_PH3 = L_G3 + 1
L_UX3 = L_PH3 + 1
L_PH4 = L_UX3 + 1
L_MASK = L_PH4 + 1
N_FACE = L_MASK + 2


def pairing(sizes, axis, first):
    spare = "gy" if axis != "gy" else "gx"
    perm = []
    real = False

    def linear(at):
        return (at["gx"] * sizes["gy"] + at["gy"]) * sizes["gz"] + at["gz"]

    for gx in range(sizes["gx"]):
        for gy in range(sizes["gy"]):
            for gz in range(sizes["gz"]):
                at = {"gx": gx, "gy": gy, "gz": gz}
                other = at[axis] + (1 if at[axis] % 2 == first else -1)
                if 0 <= other < sizes[axis]:
                    real = True
                    perm.append((linear(at), linear({**at, axis: other})))
                elif at[spare] ^ 1 < sizes[spare]:
                    perm.append((linear(at), linear({**at, spare: at[spare] ^ 1})))
    return perm if real else None


def swap(sizes, axis, send_a, send_b):
    perm_a = pairing(sizes, axis, 0)
    perm_b = pairing(sizes, axis, 1)
    got_a = lax.ppermute(send_a, AXES, perm_a) if perm_a else send_a
    got_b = lax.ppermute(send_b, AXES, perm_b) if perm_b else got_a
    return got_a, got_b


def beside(sizes, cells):
    if sizes["gy"] <= 2:
        perm = pairing(sizes, "gy", 0)
        return lax.ppermute(cells, AXES, perm) if perm else cells
    got_a, got_b = swap(sizes, "gy", cells, cells)
    even = lax.axis_index("gy") % 2 == 0
    above = jnp.where(even, got_a, got_b)
    below = jnp.where(even, got_b, got_a)
    row = lax.broadcasted_iota(jnp.int32, cells.shape, cells.ndim - 2)
    return jnp.where(row < HALO, above, below)


def relax(rho, mom, phase, grads, pops):
    inv = 1.0 / rho if rho is not None else None
    vel = [m * inv if inv is not None else m for m in mom]
    square = grads[0] * grads[0] + grads[1] * grads[1] + grads[2] * grads[2] + 0.01
    inv_mag = lax.rsqrt(square)
    mag = square * inv_mag
    out = {}
    if any(member < NF for member in pops):
        omega = 1.0 / (0.8 + 0.2 * phase)
        keep = 1.0 - omega
        scale = omega * rho
        base = scale * (1.0 - 1.5 * (vel[0] * vel[0] + vel[1] * vel[1] + vel[2] * vel[2]))
        quad_v = [4.5 * scale * v for v in vel]
        quad_g = [0.5 * inv_mag * g for g in grads]
        lin = [(3.0 * scale) * v for v in vel]
        diag = [quad_v[d] * vel[d] + quad_g[d] * grads[d] for d in range(3)]
        tail = {
            0: (1.0 / 9.0) * mag,
            1: (-0.5 / 54.0) * mag,
            2: (-0.5 / 27.0) * mag,
        }
        memo = {}

        def once(key, make):
            if key not in memo:
                memo[key] = make()
            return memo[key]

        for member in pops:
            if member >= NF:
                continue
            dims = [d for d in range(3) if VEL[member][d] != 0]
            signs = [VEL[member][d] for d in dims]
            if not dims:
                out[member] = keep * pops[member] + ((1.0 / 3.0) * base + tail[0])
                continue
            if len(dims) == 1:
                d = dims[0]
                even = once(("e", d), lambda: (1.0 / 18.0) * (base + diag[d]) + tail[1])
                odd = once(("o", d), lambda: (1.0 / 18.0) * lin[d])
                flip = signs[0]
            else:
                a, b = dims
                same = signs[0] * signs[1]
                both = once(("s", a, b), lambda: base + diag[a] + diag[b])
                mixed = once(
                    ("m", a, b),
                    lambda: 2.0 * (quad_v[a] * vel[b] + quad_g[a] * grads[b]),
                )
                even = once(
                    ("e", a, b, same),
                    lambda: (1.0 / 36.0) * (both + mixed if same > 0 else both - mixed) + tail[2],
                )
                odd = once(
                    ("o", a, b, same),
                    lambda: (1.0 / 36.0) * (lin[a] + lin[b] if same > 0 else lin[a] - lin[b]),
                )
                flip = signs[0]
            mid = keep * pops[member] + even
            out[member] = mid + odd if flip > 0 else mid - odd
    if any(member >= NF for member in pops):
        sharpen = 0.7 * (1.0 - phase * phase) * inv_mag
        part = 1.25 * 0.125
        for member in pops:
            if member < NF:
                continue
            move = VEL[member]
            if move == (0, 0, 0):
                out[member] = (1.25 * 0.25) * phase - 0.25 * pops[member]
                continue
            d = [i for i in range(3) if move[i] != 0][0]
            drift = part * (4.0 * phase * vel[d] + sharpen * grads[d])
            still = part * phase - 0.25 * pops[member]
            out[member] = still + drift if move[d] > 0 else still - drift
    return out


def moments(pops):
    rho = pops[0]
    for member in range(1, NF):
        rho = rho + pops[member]
    mom = []
    for d in range(3):
        plus = [pops[m] for m in range(NF) if VEL[m][d] > 0]
        minus = [pops[m] for m in range(NF) if VEL[m][d] < 0]
        total = plus[0] - minus[0]
        for p, m in zip(plus[1:], minus[1:]):
            total = total + (p - m)
        mom.append(total)
    return rho, mom


def add_up(values):
    total = values[0]
    for value in values[1:]:
        total = total + value
    return total


def turn(value, shift, dim):
    size = value.shape[dim]
    shift = shift % size
    return pltpu.roll(value, shift, axis=dim) if shift else value


def load_kernel(flow, phase, mask, own, out_a, out_b, mask_in, sem):
    _, cx, cy, cz = own.shape
    copies = [
        pltpu.make_async_copy(flow, own.at[pl.ds(0, NF)], sem.at[0]),
        pltpu.make_async_copy(phase, own.at[pl.ds(NF, NG)], sem.at[1]),
        pltpu.make_async_copy(mask, mask_in, sem.at[2]),
    ]
    for one in copies:
        one.start()
    for one in copies:
        one.wait()
    own[NP] = mask_in[...].astype(jnp.float32)
    even = lax.axis_index("gz") % 2 == 0
    group = lax.broadcasted_iota(jnp.int32, (cy, cz), 1) // HALO
    per = cz // (cx * HALO)
    for block in range(out_a.shape[0]):
        low = jnp.zeros((cy, cz), jnp.float32)
        high = low
        for field in range(block * per, min((block + 1) * per, NV)):
            for x in range(cx):
                value = own[field, x]
                slot = (field % per) * cx + x
                here = group == slot
                low = jnp.where(here, turn(value, slot * HALO, 1), low)
                high = jnp.where(here, turn(value, (slot + 1) * HALO, 1), high)
        out_a[block] = jnp.where(even, high, low)
        out_b[block] = jnp.where(even, low, high)


def faces_kernel(own, out_a, out_b):
    cx = own.shape[1]
    even = lax.axis_index("gx") % 2 == 0
    for out, up in ((out_a, even), (out_b, jnp.logical_not(even))):
        other = jnp.where(up, 0, 1)
        xs = [jnp.where(up, cx - 1 - d, d) for d in range(HALO)]
        for field in range(NV):
            out[field] = own[field, xs[0]]
        for member in range(NG):
            out[NV + L_G2 + member] = own[NF + member, xs[1]]
        for slot, member in enumerate(IN_F):
            out[NV + L_F2 + slot] = own[member + other, xs[1]]
        rho, mom = moments([own[member, xs[1]] for member in range(NF)])
        out[NV + L_RHO2] = rho
        for d in range(3):
            out[NV + L_MOM2 + d] = mom[d]
        out[NV + L_G3] = own[NF + IN_G + other, xs[2]]
        out[NV + L_PH3] = add_up([own[NF + member, xs[2]] for member in range(NG)])
        rho, mom = moments([own[member, xs[2]] for member in range(NF)])
        out[NV + L_UX3] = mom[0] / rho
        far = add_up([own[NF + member, xs[3]] for member in range(NG)])
        out[NV + L_PH4] = jnp.where(own[NP, xs[3]] == 1.0, far, 0.0)
        for d in range(2):
            out[NV + L_MASK + d] = own[NP, xs[1 + d]]


def strips_kernel(own, z_a, z_b, strips, *, sizes):
    _, cx, cy, cz = own.shape
    at_z = lax.axis_index("gz")
    even = at_z % 2 == 0
    group = lax.broadcasted_iota(jnp.int32, (cy, cz), 1) // HALO
    per_in = cz // (cx * HALO)
    per_out = cz // (4 * cx * HALO)
    below = [jnp.where(even, z_b[i], z_a[i]) for i in range(z_a.shape[0])]
    above = [jnp.where(even, z_a[i], z_b[i]) for i in range(z_a.shape[0])]
    has_below = at_z > 0
    has_above = at_z < sizes["gz"] - 1
    for block in range(strips.shape[0]):
        total = jnp.zeros((cy, cz), jnp.float32)
        for field in range(block * per_out, min((block + 1) * per_out, NV)):
            from_below = below[field // per_in]
            from_above = above[field // per_in]
            if field == NP:
                from_below = jnp.where(has_below, from_below, 0.0)
                from_above = jnp.where(has_above, from_above, 0.0)
            for x in range(cx):
                value = own[field, x]
                came = (field % per_in) * cx + x
                base = (field % per_out) * 4 * cx
                for piece, origin, slot in (
                    (from_below, came, base + 2 * x),
                    (value, 0, base + 2 * x + 1),
                    (value, cz // HALO - 1, base + 2 * (cx + x)),
                    (from_above, came, base + 2 * (cx + x) + 1),
                ):
                    total = jnp.where(
                        group == slot, turn(piece, (slot - origin) * HALO, 1), total
                    )
        strips[block] = total


def steps_kernel(
    own, x_a, x_b, strips, far_a, far_b,
    own_y, x_a_y, x_b_y, strips_y, far_a_y, far_b_y,
    flow_out, phase_out,
    pops, face, own_strips, far_strips, fluid, potential,
    strip_pops, strip_fluid, strip_phase, moved, stayed, strip_moved, strip_stayed,
    phase_pops, potential1, moved1, stayed1, sem,
    *, sizes,
):
    _, cx, cy, cz = flow_out.shape
    rows = 2 * cy
    at_x = lax.axis_index("gx")
    at_y = lax.axis_index("gy")
    even_x = at_x % 2 == 0
    side_a = jnp.where(even_x, 1, 0)
    side_b = 1 - side_a

    copies = []

    def copy(src, dst):
        one = pltpu.make_async_copy(src, dst, sem.at[len(copies)])
        one.start()
        copies.append(one)

    for at, (o, a, b, s, fa, fb) in (
        (0, (own, x_a, x_b, strips, far_a, far_b)),
        (cy, (own_y, x_a_y, x_b_y, strips_y, far_a_y, far_b_y)),
    ):
        part = pl.ds(at, cy)
        copy(o, pops.at[:, pl.ds(1, cx), part])
        copy(s, own_strips.at[:, part])
        for got, far, side in ((a, fa, side_a), (b, fb, side_b)):
            copy(got.at[pl.ds(0, NV)], pops.at[:, side * (cx + 1), part])
            copy(got.at[pl.ds(NV, N_FACE)], face.at[side, :, part])
            copy(far, far_strips.at[side, :, part])
    for one in copies:
        one.wait()

    lane = lax.broadcasted_iota(jnp.int32, (rows, cz), 1)
    row = lax.broadcasted_iota(jnp.int32, (rows, cz), 0)
    has_left = at_x > 0
    has_right = at_x < sizes["gx"] - 1
    has_low = at_y > 0
    has_high = at_y < sizes["gy"] - 1
    high_row = jnp.where(has_high, cy + HALO, cy)
    low_row = jnp.where(has_low, cy + HALO, rows)
    row_ok = (row < high_row) | (row >= low_row)
    has = (has_left, has_right)
    first, last = HALO, HALO + cx - 1

    def at_depth(side, depth):
        return first - depth if side == 0 else last + depth

    for x in range(cx):
        ok = (pops[NP, 1 + x] == 1.0) & row_ok
        fluid[first + x] = ok.astype(jnp.float32)
        total = add_up([pops[NF + member, 1 + x] for member in range(NG)])
        potential[first + x] = jnp.where(ok, total, 0.0)
    for side in range(2):
        side_ok = row_ok & has[side]
        for depth in range(1, HALO + 1):
            if depth == 1:
                total = add_up([pops[NF + m, side * (cx + 1)] for m in range(NG)])
            elif depth == 2:
                total = add_up([face[side, L_G2 + m] for m in range(NG)])
            else:
                total = face[side, L_PH3 if depth == 3 else L_PH4]
            ok = side_ok
            if depth < HALO:
                if depth == 1:
                    known = pops[NP, side * (cx + 1)]
                else:
                    known = face[side, L_MASK + depth - 2]
                ok = ok & (known == 1.0)
                fluid[at_depth(side, depth)] = ok.astype(jnp.float32)
            potential[at_depth(side, depth)] = jnp.where(ok, total, 0.0)

    cols = 2 * HALO
    wide = cols * cx
    per = cz // (2 * wide)
    block_ok = row_ok & (
        ((lane < wide) & has_left)
        | ((lane >= wide) & (lane < 2 * wide))
        | ((lane >= 2 * wide) & (lane < 3 * wide) & has_right)
    )
    for side in range(2):
        for field in range(NV):
            block = field // per
            origin = ((field % per) * 2 + side) * wide
            left = turn(far_strips[0, block], -origin, 1)
            mine = turn(own_strips[block], wide - origin, 1)
            right = turn(far_strips[1, block], 2 * wide - origin, 1)
            value = jnp.where(lane < wide, left, jnp.where(lane < 2 * wide, mine, right))
            if field < NP:
                strip_pops[side, field] = value
            else:
                strip_fluid[side] = jnp.where(block_ok, value, 0.0)

    def strip_grads(values):
        return (
            0.5 * (turn(values, -cols, 1) - turn(values, cols, 1)),
            0.5 * (turn(values, -1, 0) - turn(values, 1, 0)),
            0.5 * (turn(values, -1, 1) - turn(values, 1, 1)),
        )

    def push_strip(member, value, ok):
        move = VEL[member]
        value = jnp.where(ok, value, ROCK)
        value = turn(value, move[0] * cols + move[2], 1)
        return turn(value, move[1], 0)

    def strip_to_lane(side, values, at):
        if side == 0:
            return pltpu.roll(values, (2 * cz - (at * cols + HALO)) % cz, axis=1)
        return pltpu.roll(values, (cz - HALO - at * cols) % cz, axis=1)

    def main_grads(source, strip_source, at):
        here = source[at]
        down = jnp.where(lane == 0, strip_to_lane(0, strip_source[0], at), turn(here, 1, 1))
        up = jnp.where(
            lane == cz - 1, strip_to_lane(1, strip_source[1], at), turn(here, -1, 1)
        )
        return (
            0.5 * (source[at + 1] - source[at - 1]),
            0.5 * (turn(here, -1, 0) - turn(here, 1, 0)),
            0.5 * (up - down),
        )

    def push_main(member, value, ok, strip_source, at):
        move = VEL[member]
        value = jnp.where(ok, value, ROCK)
        value = turn(value, move[1], 0)
        if move[2] > 0:
            value = jnp.where(
                lane == 0, strip_to_lane(0, strip_source[0, member], at + move[0]), turn(value, 1, 1)
            )
        elif move[2] < 0:
            value = jnp.where(
                lane == cz - 1,
                strip_to_lane(1, strip_source[1, member], at + move[0]),
                turn(value, -1, 1),
            )
        return value

    for side in range(2):
        ok = strip_fluid[side] == 1.0
        values = [strip_pops[side, member] for member in range(NP)]
        total = jnp.where(ok, add_up(values[NF:]), 0.0)
        strip_phase[side] = turn(total, 1 if side == 0 else -1, 1)
        rho, mom = moments(values)
        done = relax(rho, mom, total, strip_grads(total), dict(enumerate(values)))
        for member in range(NP):
            strip_stayed[side, member] = done[member]
            strip_moved[side, member] = push_strip(member, done[member], ok)

    def collide(j, carry):
        at = first - 1 + j
        values = [pops[member, j] for member in range(NP)]
        ok = fluid[at] == 1.0
        rho, mom = moments(values)
        done = relax(
            rho, mom, potential[at], main_grads(potential, strip_phase, at),
            dict(enumerate(values)),
        )
        for member in range(NP):
            stayed[member, at] = done[member]
            moved[member, at] = push_main(member, done[member], ok, strip_moved, at)
        return carry

    lax.fori_loop(0, cx + 2, collide, 0)
    for side in range(2):
        at = at_depth(side, 2)
        members = {m + side: face[side, L_F2 + slot] for slot, m in enumerate(IN_F)}
        members.update({NF + m: face[side, L_G2 + m] for m in range(NG)})
        done = relax(
            face[side, L_RHO2], [face[side, L_MOM2 + d] for d in range(3)],
            potential[at], main_grads(potential, strip_phase, at), members,
        )
        ok = fluid[at] == 1.0
        for member in done:
            stayed[member, at] = done[member]
            moved[member, at] = push_main(member, done[member], ok, strip_moved, at)
        at = at_depth(side, 3)
        member = NF + IN_G + side
        done = relax(
            None, [face[side, L_UX3]] * 3, potential[at],
            main_grads(potential, strip_phase, at), {member: face[side, L_G3]},
        )
        ok = fluid[at] == 1.0
        moved[member, at] = push_main(member, done[member], ok, strip_moved, at)

    def pull(source, kept, member, at):
        if VEL[member] == (0, 0, 0):
            return kept[member, at]
        value = source[member, at - VEL[member][0]]
        return jnp.where(value == ROCK, kept[OPP[member], at], value)

    def stream(j, carry):
        at = first - 2 + j
        values = [pull(moved, stayed, NF + member, at) for member in range(NG)]
        for member in range(NG):
            phase_pops[member, at] = values[member]
        potential1[at] = jnp.where(fluid[at] == 1.0, add_up(values), 0.0)
        return carry

    lax.fori_loop(0, cx + 4, stream, 0)

    for side in range(2):
        ok = strip_fluid[side] == 1.0
        values = []
        for member in range(NP):
            value = strip_moved[side, member]
            back = strip_stayed[side, OPP[member]]
            values.append(jnp.where(value == ROCK, back, value))
        total = jnp.where(ok, add_up(values[NF:]), 0.0)
        rho, mom = moments(values)
        sign = 1 if side == 0 else -1
        wanted = {m: values[m] for m in range(NP) if VEL[m][2] == sign}
        done = relax(rho, mom, total, strip_grads(total), wanted)
        for member in wanted:
            strip_pops[side, member] = push_strip(member, done[member], ok)
        strip_phase[side] = turn(total, sign, 1)

    def collide1(j, carry):
        at = first - 1 + j
        values = [pull(moved, stayed, member, at) for member in range(NF)]
        values += [phase_pops[member, at] for member in range(NG)]
        ok = fluid[at] == 1.0
        rho, mom = moments(values)
        done = relax(
            rho, mom, potential1[at], main_grads(potential1, strip_phase, at),
            dict(enumerate(values)),
        )
        for member in range(NP):
            stayed1[member, at] = done[member]
            moved1[member, at] = push_main(member, done[member], ok, strip_pops, at)
        return carry

    lax.fori_loop(0, cx + 2, collide1, 0)

    def finish(x, carry):
        at = first + x
        own = pl.ds(0, cy)
        ok = fluid[at, own] == 1.0
        for member in range(NP):
            if VEL[member] == (0, 0, 0):
                value = stayed1[member, at, own]
            else:
                value = moved1[member, at - VEL[member][0], own]
                value = jnp.where(value == ROCK, stayed1[OPP[member], at, own], value)
            value = jnp.where(ok, value, pops[member, 1 + x, own])
            if member < NF:
                flow_out[member, x] = value
            else:
                phase_out[member - NF, x] = value
        return carry

    lax.fori_loop(0, cx, finish, 0)


def shards(sizes, flow_pops, phase_pops, pore_mask):
    cx, cy, cz = pore_mask.shape
    rows = 2 * cy
    assert cx >= HALO and cy == 2 * HALO and 6 * cx * HALO <= cz
    f32 = jnp.float32
    vmem = pl.BlockSpec(memory_space=pltpu.VMEM)
    anywhere = pl.BlockSpec(memory_space=pl.ANY)

    def near(*arrays):
        return [pltpu.with_memory_space_constraint(a, pltpu.VMEM) for a in arrays]

    def call(kernel, out_shape, in_specs, args, scratch=()):
        return pl.pallas_call(
            kernel,
            out_shape=out_shape,
            in_specs=in_specs,
            out_specs=jax.tree.map(lambda _: vmem, out_shape),
            scratch_shapes=scratch,
        )(*args)

    z_blocks = pl.cdiv(NV, cz // (cx * HALO))
    z_shape = pltpu.VMEM((z_blocks, cy, cz), f32)
    own, z_a, z_b = call(
        load_kernel, (pltpu.VMEM((NV, cx, cy, cz), f32), z_shape, z_shape),
        [anywhere] * 3, (flow_pops, phase_pops, pore_mask),
        [pltpu.VMEM(pore_mask.shape, jnp.int32), pltpu.SemaphoreType.DMA((3,))],
    )
    z_a, z_b = swap(sizes, "gz", z_a, z_b)

    x_shape = pltpu.VMEM((NV + N_FACE, cy, cz), f32)
    x_a, x_b = call(faces_kernel, (x_shape, x_shape), [vmem], near(own))
    x_a, x_b = swap(sizes, "gx", x_a, x_b)
    own_y = beside(sizes, own)
    x_a_y = beside(sizes, x_a)
    x_b_y = beside(sizes, x_b)

    strip_blocks = pl.cdiv(NV, cz // (4 * cx * HALO))
    strips = call(
        lambda *refs: strips_kernel(*refs, sizes=sizes),
        pltpu.VMEM((strip_blocks, cy, cz), f32), [vmem] * 3, near(own, z_a, z_b),
    )
    strips_y = beside(sizes, strips)
    far_a, far_b = swap(sizes, "gx", strips, strips)
    far_a_y = beside(sizes, far_a)
    far_b_y = beside(sizes, far_b)

    deep = cx + 2 * HALO

    def block(*lead):
        return pltpu.VMEM((*lead, rows, cz), f32)

    return call(
        lambda *refs: steps_kernel(*refs, sizes=sizes),
        (
            jax.ShapeDtypeStruct(flow_pops.shape, f32),
            jax.ShapeDtypeStruct(phase_pops.shape, f32),
        ),
        [anywhere] * 12,
        near(
            own, x_a, x_b, strips, far_a, far_b,
            own_y, x_a_y, x_b_y, strips_y, far_a_y, far_b_y,
        ),
        [
            block(NV, cx + 2),
            block(2, N_FACE),
            block(strip_blocks),
            block(2, strip_blocks),
            block(deep),
            block(deep),
            block(2, NP),
            block(2),
            block(2),
            block(NP, deep),
            block(NP, deep),
            block(2, NP),
            block(2, NP),
            block(NG, deep),
            block(deep),
            block(NP, deep),
            block(NP, deep),
            pltpu.SemaphoreType.DMA((16,)),
        ],
    )


def solution(mesh):
    sizes = dict(mesh.shape)
    placed = (P(None, "gx", "gy", "gz"), P(None, "gx", "gy", "gz"), P("gx", "gy", "gz"))
    return jax.shard_map(
        lambda *args: shards(sizes, *args),
        mesh=mesh,
        in_specs=placed,
        out_specs=(P(None, "gx", "gy", "gz"), P(None, "gx", "gy", "gz")),
        check_vma=False,
    )
```

```python
import jax
import jax.numpy as jnp
from jax import lax
from jax.experimental import pallas as pl
from jax.experimental.pallas import tpu as pltpu
from jax.sharding import PartitionSpec as P


AXES = ("gx", "gy", "gz")

VEL_F = [
    (0, 0, 0),
    (1, 0, 0),
    (-1, 0, 0),
    (0, 1, 0),
    (0, -1, 0),
    (0, 0, 1),
    (0, 0, -1),
    (1, 1, 0),
    (-1, -1, 0),
    (1, -1, 0),
    (-1, 1, 0),
    (1, 0, 1),
    (-1, 0, -1),
    (1, 0, -1),
    (-1, 0, 1),
    (0, 1, 1),
    (0, -1, -1),
    (0, 1, -1),
    (0, -1, 1),
]
OPP_F = [0, 2, 1, 4, 3, 6, 5, 8, 7, 10, 9, 12, 11, 14, 13, 16, 15, 18, 17]
NF = 19
NG = 7
NP = NF + NG
VEL = VEL_F + VEL_F[:NG]
OPP = OPP_F + [NF + other for other in OPP_F[:NG]]

HALO = 4
ROCK = 3.0e38

IN_F = [1, 7, 9, 11, 13]
IN_G = 1
NV = NP + 1
L_G2 = 0
L_F2 = L_G2 + NG
L_RHO2 = L_F2 + len(IN_F)
L_MOM2 = L_RHO2 + 1
L_G3 = L_MOM2 + 3
L_PH3 = L_G3 + 1
L_UX3 = L_PH3 + 1
L_PH4 = L_UX3 + 1
L_MASK = L_PH4 + 1
N_FACE = L_MASK + 2


def pairing(sizes, axis, first):
    spare = "gy" if axis != "gy" else "gx"
    perm = []
    real = False

    def linear(at):
        return (at["gx"] * sizes["gy"] + at["gy"]) * sizes["gz"] + at["gz"]

    for gx in range(sizes["gx"]):
        for gy in range(sizes["gy"]):
            for gz in range(sizes["gz"]):
                at = {"gx": gx, "gy": gy, "gz": gz}
                other = at[axis] + (1 if at[axis] % 2 == first else -1)
                if 0 <= other < sizes[axis]:
                    real = True
                    perm.append((linear(at), linear({**at, axis: other})))
                elif at[spare] ^ 1 < sizes[spare]:
                    perm.append((linear(at), linear({**at, spare: at[spare] ^ 1})))
    return perm if real else None


def swap(sizes, axis, send_a, send_b):
    perm_a = pairing(sizes, axis, 0)
    perm_b = pairing(sizes, axis, 1)
    got_a = lax.ppermute(send_a, AXES, perm_a) if perm_a else send_a
    got_b = lax.ppermute(send_b, AXES, perm_b) if perm_b else got_a
    return got_a, got_b


def beside(sizes, cells):
    if sizes["gy"] <= 2:
        perm = pairing(sizes, "gy", 0)
        return lax.ppermute(cells, AXES, perm) if perm else cells
    got_a, got_b = swap(sizes, "gy", cells, cells)
    even = lax.axis_index("gy") % 2 == 0
    above = jnp.where(even, got_a, got_b)
    below = jnp.where(even, got_b, got_a)
    row = lax.broadcasted_iota(jnp.int32, cells.shape, cells.ndim - 2)
    return jnp.where(row < HALO, above, below)


def relax(rho, mom, phase, grads, pops):
    inv = 1.0 / rho if rho is not None else None
    vel = [m * inv if inv is not None else m for m in mom]
    square = grads[0] * grads[0] + grads[1] * grads[1] + grads[2] * grads[2] + 0.01
    inv_mag = lax.rsqrt(square)
    mag = square * inv_mag
    out = {}
    if any(member < NF for member in pops):
        omega = 1.0 / (0.8 + 0.2 * phase)
        keep = 1.0 - omega
        scale = omega * rho
        base = scale * (1.0 - 1.5 * (vel[0] * vel[0] + vel[1] * vel[1] + vel[2] * vel[2]))
        quad_v = [4.5 * scale * v for v in vel]
        quad_g = [0.5 * inv_mag * g for g in grads]
        lin = [(3.0 * scale) * v for v in vel]
        diag = [quad_v[d] * vel[d] + quad_g[d] * grads[d] for d in range(3)]
        tail = {
            0: (1.0 / 9.0) * mag,
            1: (-0.5 / 54.0) * mag,
            2: (-0.5 / 27.0) * mag,
        }
        memo = {}

        def once(key, make):
            if key not in memo:
                memo[key] = make()
            return memo[key]

        for member in pops:
            if member >= NF:
                continue
            dims = [d for d in range(3) if VEL[member][d] != 0]
            signs = [VEL[member][d] for d in dims]
            if not dims:
                out[member] = keep * pops[member] + ((1.0 / 3.0) * base + tail[0])
                continue
            if len(dims) == 1:
                d = dims[0]
                even = once(("e", d), lambda: (1.0 / 18.0) * (base + diag[d]) + tail[1])
                odd = once(("o", d), lambda: (1.0 / 18.0) * lin[d])
                flip = signs[0]
            else:
                a, b = dims
                same = signs[0] * signs[1]
                both = once(("s", a, b), lambda: base + diag[a] + diag[b])
                mixed = once(
                    ("m", a, b),
                    lambda: 2.0 * (quad_v[a] * vel[b] + quad_g[a] * grads[b]),
                )
                even = once(
                    ("e", a, b, same),
                    lambda: (1.0 / 36.0) * (both + mixed if same > 0 else both - mixed) + tail[2],
                )
                odd = once(
                    ("o", a, b, same),
                    lambda: (1.0 / 36.0) * (lin[a] + lin[b] if same > 0 else lin[a] - lin[b]),
                )
                flip = signs[0]
            mid = keep * pops[member] + even
            out[member] = mid + odd if flip > 0 else mid - odd
    if any(member >= NF for member in pops):
        sharpen = 0.7 * (1.0 - phase * phase) * inv_mag
        part = 1.25 * 0.125
        for member in pops:
            if member < NF:
                continue
            move = VEL[member]
            if move == (0, 0, 0):
                out[member] = (1.25 * 0.25) * phase - 0.25 * pops[member]
                continue
            d = [i for i in range(3) if move[i] != 0][0]
            drift = part * (4.0 * phase * vel[d] + sharpen * grads[d])
            still = part * phase - 0.25 * pops[member]
            out[member] = still + drift if move[d] > 0 else still - drift
    return out


def moments(pops):
    rho = pops[0]
    for member in range(1, NF):
        rho = rho + pops[member]
    mom = []
    for d in range(3):
        plus = [pops[m] for m in range(NF) if VEL[m][d] > 0]
        minus = [pops[m] for m in range(NF) if VEL[m][d] < 0]
        total = plus[0] - minus[0]
        for p, m in zip(plus[1:], minus[1:]):
            total = total + (p - m)
        mom.append(total)
    return rho, mom


def add_up(values):
    total = values[0]
    for value in values[1:]:
        total = total + value
    return total


def turn(value, shift, dim):
    size = value.shape[dim]
    shift = shift % size
    return pltpu.roll(value, shift, axis=dim) if shift else value


def load_kernel(flow, phase, mask, own, out_a, out_b, mask_in, sem):
    _, cx, cy, cz = own.shape
    copies = [
        pltpu.make_async_copy(flow, own.at[pl.ds(0, NF)], sem.at[0]),
        pltpu.make_async_copy(phase, own.at[pl.ds(NF, NG)], sem.at[1]),
        pltpu.make_async_copy(mask, mask_in, sem.at[2]),
    ]
    for one in copies:
        one.start()
    for one in copies:
        one.wait()
    own[NP] = mask_in[...].astype(jnp.float32)
    even = lax.axis_index("gz") % 2 == 0
    group = lax.broadcasted_iota(jnp.int32, (cy, cz), 1) // HALO
    per = cz // (cx * HALO)
    for block in range(out_a.shape[0]):
        low = jnp.zeros((cy, cz), jnp.float32)
        high = low
        for field in range(block * per, min((block + 1) * per, NV)):
            for x in range(cx):
                value = own[field, x]
                slot = (field % per) * cx + x
                here = group == slot
                low = jnp.where(here, turn(value, slot * HALO, 1), low)
                high = jnp.where(here, turn(value, (slot + 1) * HALO, 1), high)
        out_a[block] = jnp.where(even, high, low)
        out_b[block] = jnp.where(even, low, high)


def faces_kernel(own, out_a, out_b):
    cx = own.shape[1]
    even = lax.axis_index("gx") % 2 == 0
    for out, up in ((out_a, even), (out_b, jnp.logical_not(even))):
        other = jnp.where(up, 0, 1)
        xs = [jnp.where(up, cx - 1 - d, d) for d in range(HALO)]
        for field in range(NV):
            out[field] = own[field, xs[0]]
        for member in range(NG):
            out[NV + L_G2 + member] = own[NF + member, xs[1]]
        for slot, member in enumerate(IN_F):
            out[NV + L_F2 + slot] = own[member + other, xs[1]]
        rho, mom = moments([own[member, xs[1]] for member in range(NF)])
        out[NV + L_RHO2] = rho
        for d in range(3):
            out[NV + L_MOM2 + d] = mom[d]
        out[NV + L_G3] = own[NF + IN_G + other, xs[2]]
        out[NV + L_PH3] = add_up([own[NF + member, xs[2]] for member in range(NG)])
        rho, mom = moments([own[member, xs[2]] for member in range(NF)])
        out[NV + L_UX3] = mom[0] / rho
        far = add_up([own[NF + member, xs[3]] for member in range(NG)])
        out[NV + L_PH4] = jnp.where(own[NP, xs[3]] == 1.0, far, 0.0)
        for d in range(2):
            out[NV + L_MASK + d] = own[NP, xs[1 + d]]


def strips_kernel(own, z_a, z_b, strips, *, sizes):
    _, cx, cy, cz = own.shape
    at_z = lax.axis_index("gz")
    even = at_z % 2 == 0
    group = lax.broadcasted_iota(jnp.int32, (cy, cz), 1) // HALO
    per_in = cz // (cx * HALO)
    per_out = cz // (4 * cx * HALO)
    below = [jnp.where(even, z_b[i], z_a[i]) for i in range(z_a.shape[0])]
    above = [jnp.where(even, z_a[i], z_b[i]) for i in range(z_a.shape[0])]
    has_below = at_z > 0
    has_above = at_z < sizes["gz"] - 1
    for block in range(strips.shape[0]):
        total = jnp.zeros((cy, cz), jnp.float32)
        for field in range(block * per_out, min((block + 1) * per_out, NV)):
            from_below = below[field // per_in]
            from_above = above[field // per_in]
            if field == NP:
                from_below = jnp.where(has_below, from_below, 0.0)
                from_above = jnp.where(has_above, from_above, 0.0)
            for x in range(cx):
                value = own[field, x]
                came = (field % per_in) * cx + x
                base = (field % per_out) * 4 * cx
                for piece, origin, slot in (
                    (from_below, came, base + 2 * x),
                    (value, 0, base + 2 * x + 1),
                    (value, cz // HALO - 1, base + 2 * (cx + x)),
                    (from_above, came, base + 2 * (cx + x) + 1),
                ):
                    total = jnp.where(
                        group == slot, turn(piece, (slot - origin) * HALO, 1), total
                    )
        strips[block] = total


def steps_kernel(
    own, x_a, x_b, strips, far_a, far_b,
    own_y, x_a_y, x_b_y, strips_y, far_a_y, far_b_y,
    flow_out, phase_out,
    face, fluid, potential,
    strip_pops, strip_fluid, strip_phase, moved, stayed, strip_moved, strip_stayed,
    phase_pops, potential1, moved1, stayed1, result, sem,
    *, sizes,
):
    _, cx, cy, cz = own.shape
    rows = 2 * cy
    at_x = lax.axis_index("gx")
    at_y = lax.axis_index("gy")
    even_x = at_x % 2 == 0
    first, last = HALO, HALO + cx - 1
    own_rows = pl.ds(0, cy)

    def whole(cells, cells_y, *at):
        return jnp.concatenate([cells[at], cells_y[at]], axis=0)

    lane = lax.broadcasted_iota(jnp.int32, (rows, cz), 1)
    row = lax.broadcasted_iota(jnp.int32, (rows, cz), 0)
    has_left = at_x > 0
    has_right = at_x < sizes["gx"] - 1
    has_low = at_y > 0
    has_high = at_y < sizes["gy"] - 1
    high_row = jnp.where(has_high, cy + HALO, cy)
    low_row = jnp.where(has_low, cy + HALO, rows)
    row_ok = (row < high_row) | (row >= low_row)
    has = (has_left, has_right)

    def at_depth(side, depth):
        return first - depth if side == 0 else last + depth

    side_a = jnp.where(even_x, 1, 0)
    ends = ((x_a, x_a_y, side_a), (x_b, x_b_y, 1 - side_a))

    for x in range(cx):
        ok = (whole(own, own_y, NP, x) == 1.0) & row_ok
        fluid[first + x] = ok.astype(jnp.float32)
        total = add_up([whole(own, own_y, NF + member, x) for member in range(NG)])
        potential[first + x] = jnp.where(ok, total, 0.0)
    for got, got_y, side in ends:
        for layer in range(N_FACE):
            face[side, layer] = whole(got, got_y, NV + layer)
        at = jnp.where(side == 0, first - 1, last + 1)
        side_ok = row_ok & ((side == 0) & has_left | (side == 1) & has_right)
        ok = side_ok & (whole(got, got_y, NP) == 1.0)
        total = add_up([whole(got, got_y, NF + member) for member in range(NG)])
        fluid[at] = ok.astype(jnp.float32)
        potential[at] = jnp.where(ok, total, 0.0)
    for side in range(2):
        side_ok = row_ok & has[side]
        for depth in range(2, HALO + 1):
            at = at_depth(side, depth)
            ok = side_ok
            if depth == 2:
                total = add_up([face[side, L_G2 + m] for m in range(NG)])
            else:
                total = face[side, L_PH3 if depth == 3 else L_PH4]
            if depth < HALO:
                ok = ok & (face[side, L_MASK + depth - 2] == 1.0)
                fluid[at] = ok.astype(jnp.float32)
            potential[at] = jnp.where(ok, total, 0.0)

    cols = 2 * HALO
    wide = cols * cx
    per = cz // (2 * wide)
    block_ok = row_ok & (
        ((lane < wide) & has_left)
        | ((lane >= wide) & (lane < 2 * wide))
        | ((lane >= 2 * wide) & (lane < 3 * wide) & has_right)
    )
    for block in range(strips.shape[0]):
        mine = whole(strips, strips_y, block)
        from_a = whole(far_a, far_a_y, block)
        from_b = whole(far_b, far_b_y, block)
        left = jnp.where(even_x, from_b, from_a)
        right = jnp.where(even_x, from_a, from_b)
        for field in range(block * per, min((block + 1) * per, NV)):
            for side in range(2):
                origin = ((field % per) * 2 + side) * wide
                value = jnp.where(
                    lane < wide,
                    turn(left, -origin, 1),
                    jnp.where(
                        lane < 2 * wide,
                        turn(mine, wide - origin, 1),
                        turn(right, 2 * wide - origin, 1),
                    ),
                )
                if field < NP:
                    strip_pops[side, field] = value
                else:
                    strip_fluid[side] = jnp.where(block_ok, value, 0.0)

    def strip_grads(values):
        return (
            0.5 * (turn(values, -cols, 1) - turn(values, cols, 1)),
            0.5 * (turn(values, -1, 0) - turn(values, 1, 0)),
            0.5 * (turn(values, -1, 1) - turn(values, 1, 1)),
        )

    def push_strip(member, value, ok):
        move = VEL[member]
        value = jnp.where(ok, value, ROCK)
        value = turn(value, move[0] * cols + move[2], 1)
        return turn(value, move[1], 0)

    def strip_to_lane(side, values, at):
        if side == 0:
            return pltpu.roll(values, (2 * cz - (at * cols + HALO)) % cz, axis=1)
        return pltpu.roll(values, (cz - HALO - at * cols) % cz, axis=1)

    def main_grads(source, strip_source, at):
        here = source[at]
        down = jnp.where(lane == 0, strip_to_lane(0, strip_source[0], at), turn(here, 1, 1))
        up = jnp.where(
            lane == cz - 1, strip_to_lane(1, strip_source[1], at), turn(here, -1, 1)
        )
        return (
            0.5 * (source[at + 1] - source[at - 1]),
            0.5 * (turn(here, -1, 0) - turn(here, 1, 0)),
            0.5 * (up - down),
        )

    def push_z(member, value, strip_source, at, part):
        move = VEL[member]
        size = value.shape[0]
        if move[2] > 0:
            fill = strip_to_lane(0, strip_source[0, member, part], at + move[0])
            return jnp.where(lane[:size] == 0, fill, turn(value, 1, 1))
        if move[2] < 0:
            fill = strip_to_lane(1, strip_source[1, member, part], at + move[0])
            return jnp.where(lane[:size] == cz - 1, fill, turn(value, -1, 1))
        return value

    def push_main(member, value, ok, at):
        value = turn(jnp.where(ok, value, ROCK), VEL[member][1], 0)
        return push_z(member, value, strip_moved, at, pl.ds(0, rows))

    for side in range(2):
        ok = strip_fluid[side] == 1.0
        values = [strip_pops[side, member] for member in range(NP)]
        total = jnp.where(ok, add_up(values[NF:]), 0.0)
        strip_phase[side] = turn(total, 1 if side == 0 else -1, 1)
        rho, mom = moments(values)
        done = relax(rho, mom, total, strip_grads(total), dict(enumerate(values)))
        for member in range(NP):
            strip_stayed[side, member] = done[member]
            strip_moved[side, member] = push_strip(member, done[member], ok)

    def collide(at, values):
        ok = fluid[at] == 1.0
        rho, mom = moments(values)
        grads = main_grads(potential, strip_phase, at)
        done = relax(rho, mom, potential[at], grads, dict(enumerate(values)))
        for member in range(NP):
            stayed[member, at] = done[member]
            moved[member, at] = push_main(member, done[member], ok, at)

    def collide_own(x, carry):
        collide(first + x, [whole(own, own_y, member, x) for member in range(NP)])
        return carry

    lax.fori_loop(0, cx, collide_own, 0, unroll=True)
    for got, got_y, side in ends:
        collide(
            jnp.where(side == 0, first - 1, last + 1),
            [whole(got, got_y, member) for member in range(NP)],
        )
    for side in range(2):
        at = at_depth(side, 2)
        members = {m + side: face[side, L_F2 + slot] for slot, m in enumerate(IN_F)}
        members.update({NF + m: face[side, L_G2 + m] for m in range(NG)})
        done = relax(
            face[side, L_RHO2], [face[side, L_MOM2 + d] for d in range(3)],
            potential[at], main_grads(potential, strip_phase, at), members,
        )
        ok = fluid[at] == 1.0
        for member in done:
            stayed[member, at] = done[member]
            moved[member, at] = push_main(member, done[member], ok, at)
        at = at_depth(side, 3)
        member = NF + IN_G + side
        done = relax(
            None, [face[side, L_UX3]] * 3, potential[at],
            main_grads(potential, strip_phase, at), {member: face[side, L_G3]},
        )
        ok = fluid[at] == 1.0
        moved[member, at] = push_main(member, done[member], ok, at)

    def pull(member, at, part):
        if VEL[member] == (0, 0, 0):
            return stayed[member, at, part]
        value = moved[member, at - VEL[member][0], part]
        return jnp.where(value == ROCK, stayed[OPP[member], at, part], value)

    def stream(j, carry):
        at = first - 2 + j
        values = [pull(NF + member, at, pl.ds(0, rows)) for member in range(NG)]
        for member in range(NG):
            phase_pops[member, at] = values[member]
        potential1[at] = jnp.where(fluid[at] == 1.0, add_up(values), 0.0)
        return carry

    lax.fori_loop(0, cx + 4, stream, 0, unroll=True)

    for side in range(2):
        ok = strip_fluid[side] == 1.0
        values = []
        for member in range(NP):
            value = strip_moved[side, member]
            back = strip_stayed[side, OPP[member]]
            values.append(jnp.where(value == ROCK, back, value))
        total = jnp.where(ok, add_up(values[NF:]), 0.0)
        rho, mom = moments(values)
        sign = 1 if side == 0 else -1
        wanted = {m: values[m] for m in range(NP) if VEL[m][2] == sign}
        done = relax(rho, mom, total, strip_grads(total), wanted)
        for member in wanted:
            strip_pops[side, member] = push_strip(member, done[member], ok)
        strip_phase[side] = turn(total, sign, 1)

    def collide1(at, wanted, keep):
        grads = main_grads(potential1, strip_phase, at)
        halves = []
        for half in range(2):
            part = pl.ds(half * cy, cy)
            values = [pull(member, at, part) for member in range(NF)]
            values += [phase_pops[member, at, part] for member in range(NG)]
            rho, mom = moments(values)
            members = [m for m in wanted if half == 0 or VEL[m][1] != 0]
            done = relax(
                rho, mom, potential1[at, part],
                [g[half * cy : (half + 1) * cy] for g in grads],
                {m: values[m] for m in members},
            )
            halves.append((done, fluid[at, part] == 1.0))
        (done, ok), (done_y, ok_y) = halves
        for member in wanted:
            if keep:
                stayed1[member, at] = done[member]
            step_y = VEL[member][1]
            value = turn(jnp.where(ok, done[member], ROCK), step_y, 0)
            if step_y:
                value_y = turn(jnp.where(ok_y, done_y[member], ROCK), step_y, 0)
                edge = 0 if step_y > 0 else cy - 1
                value = jnp.where(row[:cy] == edge, value_y, value)
            moved1[member, at] = push_z(member, value, strip_pops, at, own_rows)

    def collide1_own(x, carry):
        collide1(first + x, range(NP), True)
        return carry

    lax.fori_loop(0, cx, collide1_own, 0, unroll=True)
    for side in range(2):
        inward = 1 if side == 0 else -1
        collide1(at_depth(side, 1), [m for m in range(NP) if VEL[m][0] == inward], False)

    def outputs(x):
        return (
            pltpu.make_async_copy(
                result.at[pl.ds(0, NF), x], flow_out.at[:, x], sem.at[0, x]
            ),
            pltpu.make_async_copy(
                result.at[pl.ds(NF, NG), x], phase_out.at[:, x], sem.at[1, x]
            ),
        )

    def finish(x, carry):
        at = first + x
        ok = fluid[at, own_rows] == 1.0
        for member in range(NP):
            if VEL[member] == (0, 0, 0):
                value = stayed1[member, at]
            else:
                value = moved1[member, at - VEL[member][0]]
                value = jnp.where(value == ROCK, stayed1[OPP[member], at], value)
            result[member, x] = jnp.where(ok, value, own[member, x])
        for one in outputs(x):
            one.start()
        return carry

    lax.fori_loop(0, cx, finish, 0, unroll=True)
    for x in range(cx):
        for one in outputs(x):
            one.wait()


def shards(sizes, flow_pops, phase_pops, pore_mask):
    cx, cy, cz = pore_mask.shape
    rows = 2 * cy
    assert cx >= HALO and cy == 2 * HALO and 6 * cx * HALO <= cz
    f32 = jnp.float32
    vmem = pl.BlockSpec(memory_space=pltpu.VMEM)
    anywhere = pl.BlockSpec(memory_space=pl.ANY)

    def near(*arrays):
        return [pltpu.with_memory_space_constraint(a, pltpu.VMEM) for a in arrays]

    def call(kernel, out_shape, in_specs, args, scratch=(), out_specs=None):
        return pl.pallas_call(
            kernel,
            out_shape=out_shape,
            in_specs=in_specs,
            out_specs=out_specs or jax.tree.map(lambda _: vmem, out_shape),
            scratch_shapes=scratch,
        )(*args)

    z_blocks = pl.cdiv(NV, cz // (cx * HALO))
    z_shape = pltpu.VMEM((z_blocks, cy, cz), f32)
    own, z_a, z_b = call(
        load_kernel, (pltpu.VMEM((NV, cx, cy, cz), f32), z_shape, z_shape),
        [anywhere] * 3, (flow_pops, phase_pops, pore_mask),
        [pltpu.VMEM(pore_mask.shape, jnp.int32), pltpu.SemaphoreType.DMA((3,))],
    )
    z_a, z_b = swap(sizes, "gz", z_a, z_b)

    x_shape = pltpu.VMEM((NV + N_FACE, cy, cz), f32)
    x_a, x_b = call(faces_kernel, (x_shape, x_shape), [vmem], near(own))
    x_a, x_b = swap(sizes, "gx", x_a, x_b)
    own_y = beside(sizes, own)
    x_a_y = beside(sizes, x_a)
    x_b_y = beside(sizes, x_b)

    strip_blocks = pl.cdiv(NV, cz // (4 * cx * HALO))
    strips = call(
        lambda *refs: strips_kernel(*refs, sizes=sizes),
        pltpu.VMEM((strip_blocks, cy, cz), f32), [vmem] * 3, near(own, z_a, z_b),
    )
    strips_y = beside(sizes, strips)
    far_a, far_b = swap(sizes, "gx", strips, strips)
    far_a_y = beside(sizes, far_a)
    far_b_y = beside(sizes, far_b)

    deep = cx + 2 * HALO

    def block(*lead):
        return pltpu.VMEM((*lead, rows, cz), f32)

    return call(
        lambda *refs: steps_kernel(*refs, sizes=sizes),
        (
            jax.ShapeDtypeStruct(flow_pops.shape, f32),
            jax.ShapeDtypeStruct(phase_pops.shape, f32),
        ),
        [vmem] * 12,
        near(
            own, x_a, x_b, strips, far_a, far_b,
            own_y, x_a_y, x_b_y, strips_y, far_a_y, far_b_y,
        ),
        [
            block(2, N_FACE),
            block(deep),
            block(deep),
            block(2, NP),
            block(2),
            block(2),
            block(NP, deep),
            block(NP, deep),
            block(2, NP),
            block(2, NP),
            block(NG, deep),
            block(deep),
            pltpu.VMEM((NP, deep, cy, cz), f32),
            pltpu.VMEM((NP, deep, cy, cz), f32),
            pltpu.VMEM((NP, cx, cy, cz), f32),
            pltpu.SemaphoreType.DMA((2, cx)),
        ],
        (anywhere, anywhere),
    )


def solution(mesh):
    sizes = dict(mesh.shape)
    placed = (P(None, "gx", "gy", "gz"), P(None, "gx", "gy", "gz"), P("gx", "gy", "gz"))
    return jax.shard_map(
        lambda *args: shards(sizes, *args),
        mesh=mesh,
        in_specs=placed,
        out_specs=(P(None, "gx", "gy", "gz"), P(None, "gx", "gy", "gz")),
        check_vma=False,
    )
```

```python
import jax
import jax.numpy as jnp
from jax import lax
from jax.experimental import pallas as pl
from jax.experimental.pallas import tpu as pltpu
from jax.sharding import PartitionSpec as P


AXES = ("gx", "gy", "gz")

VEL_F = [
    (0, 0, 0),
    (1, 0, 0),
    (-1, 0, 0),
    (0, 1, 0),
    (0, -1, 0),
    (0, 0, 1),
    (0, 0, -1),
    (1, 1, 0),
    (-1, -1, 0),
    (1, -1, 0),
    (-1, 1, 0),
    (1, 0, 1),
    (-1, 0, -1),
    (1, 0, -1),
    (-1, 0, 1),
    (0, 1, 1),
    (0, -1, -1),
    (0, 1, -1),
    (0, -1, 1),
]
OPP_F = [0, 2, 1, 4, 3, 6, 5, 8, 7, 10, 9, 12, 11, 14, 13, 16, 15, 18, 17]
NF = 19
NG = 7
NP = NF + NG
VEL = VEL_F + VEL_F[:NG]
OPP = OPP_F + [NF + other for other in OPP_F[:NG]]

HALO = 4
ROCK = 3.0e38

IN_F = [1, 7, 9, 11, 13]
IN_G = 1
NV = NP + 1
L_G2 = 0
L_F2 = L_G2 + NG
L_G3 = L_F2 + len(IN_F)
L_PH3 = L_G3 + 1
L_PH4 = L_PH3 + 1
L_MASK = L_PH4 + 1
N_FACE = L_MASK + 2


def pairing(sizes, axis, first):
    spare = "gy" if axis != "gy" else "gx"
    perm = []
    real = False

    def linear(at):
        return (at["gx"] * sizes["gy"] + at["gy"]) * sizes["gz"] + at["gz"]

    for gx in range(sizes["gx"]):
        for gy in range(sizes["gy"]):
            for gz in range(sizes["gz"]):
                at = {"gx": gx, "gy": gy, "gz": gz}
                other = at[axis] + (1 if at[axis] % 2 == first else -1)
                if 0 <= other < sizes[axis]:
                    real = True
                    perm.append((linear(at), linear({**at, axis: other})))
                elif at[spare] ^ 1 < sizes[spare]:
                    perm.append((linear(at), linear({**at, spare: at[spare] ^ 1})))
    return perm if real else None


def swap(sizes, axis, send_a, send_b):
    perm_a = pairing(sizes, axis, 0)
    perm_b = pairing(sizes, axis, 1)
    got_a = lax.ppermute(send_a, AXES, perm_a) if perm_a else send_a
    got_b = lax.ppermute(send_b, AXES, perm_b) if perm_b else got_a
    return got_a, got_b


def beside(sizes, cells):
    if sizes["gy"] <= 2:
        perm = pairing(sizes, "gy", 0)
        return lax.ppermute(cells, AXES, perm) if perm else cells
    got_a, got_b = swap(sizes, "gy", cells, cells)
    even = lax.axis_index("gy") % 2 == 0
    above = jnp.where(even, got_a, got_b)
    below = jnp.where(even, got_b, got_a)
    row = lax.broadcasted_iota(jnp.int32, cells.shape, cells.ndim - 2)
    return jnp.where(row < HALO, above, below)


def relax(rho, mom, phase, grads, pops):
    inv = 1.0 / rho
    vel = [m * inv for m in mom]
    if grads is not None:
        square = grads[0] * grads[0] + grads[1] * grads[1] + grads[2] * grads[2] + 0.01
        inv_mag = lax.rsqrt(square)
        mag = square * inv_mag
    out = {}
    if any(member < NF for member in pops):
        omega = 1.0 / (0.8 + 0.2 * phase)
        keep = 1.0 - omega
        scale = omega * rho
        base = scale * (1.0 - 1.5 * (vel[0] * vel[0] + vel[1] * vel[1] + vel[2] * vel[2]))
        quad_v = [4.5 * scale * v for v in vel]
        lin = [(3.0 * scale) * v for v in vel]
        diag = [quad_v[d] * vel[d] for d in range(3)]
        tail = {0: 0.0, 1: 0.0, 2: 0.0}
        if grads is not None:
            quad_g = [0.5 * inv_mag * g for g in grads]
            diag = [diag[d] + quad_g[d] * grads[d] for d in range(3)]
            tail = {
                0: (1.0 / 9.0) * mag,
                1: (-0.5 / 54.0) * mag,
                2: (-0.5 / 27.0) * mag,
            }

        def cross(a, b):
            total = quad_v[a] * vel[b]
            if grads is not None:
                total = total + quad_g[a] * grads[b]
            return 2.0 * total

        memo = {}

        def once(key, make):
            if key not in memo:
                memo[key] = make()
            return memo[key]

        for member in pops:
            if member >= NF:
                continue
            dims = [d for d in range(3) if VEL[member][d] != 0]
            signs = [VEL[member][d] for d in dims]
            if not dims:
                out[member] = keep * pops[member] + ((1.0 / 3.0) * base + tail[0])
                continue
            if len(dims) == 1:
                d = dims[0]
                even = once(("e", d), lambda: (1.0 / 18.0) * (base + diag[d]) + tail[1])
                odd = once(("o", d), lambda: (1.0 / 18.0) * lin[d])
                flip = signs[0]
            else:
                a, b = dims
                same = signs[0] * signs[1]
                both = once(("s", a, b), lambda: base + diag[a] + diag[b])
                mixed = once(("m", a, b), lambda: cross(a, b))
                even = once(
                    ("e", a, b, same),
                    lambda: (1.0 / 36.0) * (both + mixed if same > 0 else both - mixed) + tail[2],
                )
                odd = once(
                    ("o", a, b, same),
                    lambda: (1.0 / 36.0) * (lin[a] + lin[b] if same > 0 else lin[a] - lin[b]),
                )
                flip = signs[0]
            mid = keep * pops[member] + even
            out[member] = mid + odd if flip > 0 else mid - odd
    if any(member >= NF for member in pops):
        part = 1.25 * 0.125
        if grads is not None:
            sharpen = 0.7 * (1.0 - phase * phase) * inv_mag
        for member in pops:
            if member < NF:
                continue
            move = VEL[member]
            if move == (0, 0, 0):
                out[member] = (1.25 * 0.25) * phase - 0.25 * pops[member]
                continue
            d = [i for i in range(3) if move[i] != 0][0]
            drift = 4.0 * phase * vel[d]
            if grads is not None:
                drift = drift + sharpen * grads[d]
            still = part * phase - 0.25 * pops[member]
            out[member] = still + part * drift if move[d] > 0 else still - part * drift
    return out


def relax_rest(phase, grads, pops):
    square = grads[0] * grads[0] + grads[1] * grads[1] + grads[2] * grads[2] + 0.01
    inv_mag = lax.rsqrt(square)
    mag = square * inv_mag
    half = 0.5 * inv_mag
    sharpen = (1.25 * 0.125 * 0.7) * (1.0 - phase * phase) * inv_mag
    quad = [half * g for g in grads]
    diag = [quad[d] * grads[d] for d in range(3)]
    memo = {}
    out = {}
    for member in pops:
        move = VEL[member]
        dims = [d for d in range(3) if move[d] != 0]
        if member >= NF:
            if dims:
                d = dims[0]
                if d not in memo:
                    memo[d] = sharpen * grads[d]
                out[member] = pops[member] + memo[d] if move[d] > 0 else pops[member] - memo[d]
            else:
                out[member] = pops[member]
            continue
        key = tuple(abs(v) for v in move) + (
            (move[dims[0]] * move[dims[1]],) if len(dims) == 2 else ()
        )
        if key not in memo:
            if not dims:
                memo[key] = (1.0 / 9.0) * mag
            elif len(dims) == 1:
                memo[key] = (1.0 / 18.0) * diag[dims[0]] - (0.5 / 54.0) * mag
            else:
                a, b = dims
                mixed = 2.0 * (quad[a] * grads[b])
                both = diag[a] + diag[b]
                both = both + mixed if key[3] > 0 else both - mixed
                memo[key] = (1.0 / 36.0) * both - (0.5 / 27.0) * mag
        out[member] = pops[member] + memo[key]
    return out


def moments(pops):
    rho = pops[0]
    for member in range(1, NF):
        rho = rho + pops[member]
    mom = []
    for d in range(3):
        plus = [pops[m] for m in range(NF) if VEL[m][d] > 0]
        minus = [pops[m] for m in range(NF) if VEL[m][d] < 0]
        total = plus[0] - minus[0]
        for p, m in zip(plus[1:], minus[1:]):
            total = total + (p - m)
        mom.append(total)
    return rho, mom


def add_up(values):
    total = values[0]
    for value in values[1:]:
        total = total + value
    return total


def turn(value, shift, dim):
    size = value.shape[dim]
    shift = shift % size
    return pltpu.roll(value, shift, axis=dim) if shift else value


def load_kernel(flow, phase, mask, own, cells, ends, out_a, out_b, mask_in, sem):
    _, cx, cy, cz = own.shape
    copies = [
        pltpu.make_async_copy(flow, own.at[pl.ds(0, NF)], sem.at[0]),
        pltpu.make_async_copy(phase, own.at[pl.ds(NF, NG)], sem.at[1]),
        pltpu.make_async_copy(mask, mask_in, sem.at[2]),
    ]
    for one in copies:
        one.start()
    for one in copies:
        one.wait()
    cells[NP] = mask_in[...].astype(jnp.float32)
    for x in range(cx):
        values = [own[member, x] for member in range(NP)]
        rho, mom = moments(values)
        done = relax(rho, mom, add_up(values[NF:]), None, dict(enumerate(values)))
        for member in range(NP):
            cells[member, x] = done[member]
    even = lax.axis_index("gz") % 2 == 0
    lane = lax.broadcasted_iota(jnp.int32, (cy, cz), 1)
    group = lane // (2 * HALO)
    first_half = lane % (2 * HALO) < HALO
    per = cz // (2 * HALO * cx)
    for block in range(ends.shape[0]):
        total = jnp.zeros((cy, cz), jnp.float32)
        for field in range(block * per, min((block + 1) * per, NV)):
            for x in range(cx):
                slot = (field % per) * cx + x
                value = turn(cells[field, x], slot * 2 * HALO + HALO, 1)
                total = jnp.where(group == slot, value, total)
        ends[block] = total
    for pair in range(out_a.shape[0]):
        one = ends[2 * pair]
        two = ends[min(2 * pair + 1, ends.shape[0] - 1)]
        high = jnp.where(first_half, one, turn(two, HALO, 1))
        low = jnp.where(first_half, turn(one, -HALO, 1), two)
        out_a[pair] = jnp.where(even, high, low)
        out_b[pair] = jnp.where(even, low, high)


def pack_face(own, out, base, up):
    cx = own.shape[1]
    other = jnp.where(up, 0, 1)
    xs = [jnp.where(up, cx - 1 - d, d) for d in range(HALO)]
    for field in range(NV):
        out[base + field] = own[field, xs[0]]
    base = base + NV
    for member in range(NG):
        out[base + L_G2 + member] = own[NF + member, xs[1]]
    for slot, member in enumerate(IN_F):
        out[base + L_F2 + slot] = own[member + other, xs[1]]
    out[base + L_G3] = own[NF + IN_G + other, xs[2]]
    out[base + L_PH3] = add_up([own[NF + member, xs[2]] for member in range(NG)])
    far = add_up([own[NF + member, xs[3]] for member in range(NG)])
    out[base + L_PH4] = jnp.where(own[NP, xs[3]] == 1.0, far, 0.0)
    for d in range(2):
        out[base + L_MASK + d] = own[NP, xs[1 + d]]


def faces_kernel(own, out_a, out_b):
    even = lax.axis_index("gx") % 2 == 0
    pack_face(own, out_a, 0, even)
    pack_face(own, out_b, 0, jnp.logical_not(even))


def strips_kernel(ends, z_a, z_b, strips, *, sizes):
    blocks, cy, cz = ends.shape
    at_z = lax.axis_index("gz")
    even = at_z % 2 == 0
    lane = lax.broadcasted_iota(jnp.int32, (cy, cz), 1)
    first_half = lane % (2 * HALO) < HALO
    has_below = at_z > 0
    has_above = at_z < sizes["gz"] - 1
    for block in range(blocks):
        from_a, from_b = z_a[block // 2], z_b[block // 2]
        below = jnp.where(even, from_b, from_a)
        above = jnp.where(even, from_a, from_b)
        if block % 2 == 0:
            above = turn(above, HALO, 1)
        else:
            below = turn(below, -HALO, 1)
        if block == blocks - 1:
            below = jnp.where(has_below, below, 0.0)
            above = jnp.where(has_above, above, 0.0)
        own = ends[block]
        strips[block] = jnp.where(first_half, below, own)
        strips[blocks + block] = jnp.where(first_half, own, above)


def steps_kernel(
    own, cells, cells_y, strips, strips_y, far_a, far_b, far_a_y, far_b_y,
    x_a, x_b, x_a_y, x_b_y,
    flow_out, phase_out,
    face, fluid, potential,
    strip_pops, strip_fluid, fill_moved, fill_moved1, moved, stayed, strip_moved, strip_stayed,
    phase_pops, potential1, moved1, stayed1, result, sem,
    *, sizes,
):
    _, cx, cy, cz = own.shape
    rows = 2 * cy
    at_x = lax.axis_index("gx")
    at_y = lax.axis_index("gy")
    even_x = at_x % 2 == 0
    first, last = HALO, HALO + cx - 1
    own_rows = pl.ds(0, cy)

    def whole(cells, cells_y, *at):
        return jnp.concatenate([cells[at], cells_y[at]], axis=0)

    lane = lax.broadcasted_iota(jnp.int32, (rows, cz), 1)
    row = lax.broadcasted_iota(jnp.int32, (rows, cz), 0)
    has_left = at_x > 0
    has_right = at_x < sizes["gx"] - 1
    has_low = at_y > 0
    has_high = at_y < sizes["gy"] - 1
    high_row = jnp.where(has_high, cy + HALO, cy)
    low_row = jnp.where(has_low, cy + HALO, rows)
    row_ok = (row < high_row) | (row >= low_row)
    has = (has_left, has_right)

    def at_depth(side, depth):
        return first - depth if side == 0 else last + depth

    side_a = jnp.where(even_x, 1, 0)
    ends = ((x_a, x_a_y, side_a), (x_b, x_b_y, 1 - side_a))

    def whole_face(end, layer):
        return whole(end[0], end[1], layer)

    for x in range(cx):
        ok = (whole(cells, cells_y, NP, x) == 1.0) & row_ok
        fluid[first + x] = ok.astype(jnp.float32)
        total = add_up([whole(cells, cells_y, NF + member, x) for member in range(NG)])
        potential[first + x] = jnp.where(ok, total, 0.0)
    for end in ends:
        side = end[2]
        for layer in range(N_FACE):
            face[side, layer] = whole_face(end, NV + layer)
        at = jnp.where(side == 0, first - 1, last + 1)
        side_ok = row_ok & ((side == 0) & has_left | (side == 1) & has_right)
        ok = side_ok & (whole_face(end, NP) == 1.0)
        total = add_up([whole_face(end, NF + member) for member in range(NG)])
        fluid[at] = ok.astype(jnp.float32)
        potential[at] = jnp.where(ok, total, 0.0)
    for side in range(2):
        side_ok = row_ok & has[side]
        for depth in range(2, HALO + 1):
            at = at_depth(side, depth)
            ok = side_ok
            if depth == 2:
                total = add_up([face[side, L_G2 + m] for m in range(NG)])
            else:
                total = face[side, L_PH3 if depth == 3 else L_PH4]
            if depth < HALO:
                ok = ok & (face[side, L_MASK + depth - 2] == 1.0)
                fluid[at] = ok.astype(jnp.float32)
            potential[at] = jnp.where(ok, total, 0.0)

    cols = 2 * HALO
    wide = cols * cx
    per = cz // wide
    block_ok = row_ok & (
        ((lane < wide) & has_left)
        | ((lane >= wide) & (lane < 2 * wide))
        | ((lane >= 2 * wide) & (lane < 3 * wide) & has_right)
    )
    blocks = strips.shape[0] // 2
    group = lane // wide
    for side in range(2):
        for block in range(blocks):
            at = side * blocks + block
            from_a = whole(far_a, far_a_y, at)
            from_b = whole(far_b, far_b_y, at)
            left = jnp.where(even_x, from_b, from_a)
            mine = turn(whole(strips, strips_y, at), wide, 1)
            right = turn(jnp.where(even_x, from_a, from_b), 2 * wide, 1)
            for field in range(block * per, min((block + 1) * per, NV)):
                spot = field % per
                value = jnp.where(
                    group == spot, left, jnp.where(group == (spot + 1) % per, mine, right)
                )
                value = turn(value, -spot * wide, 1)
                if field < NP:
                    strip_pops[side, field] = value
                else:
                    strip_fluid[side] = jnp.where(block_ok, value, 0.0)

    def strip_grads(values):
        return (
            0.5 * (turn(values, -cols, 1) - turn(values, cols, 1)),
            0.5 * (turn(values, -1, 0) - turn(values, 1, 0)),
            0.5 * (turn(values, -1, 1) - turn(values, 1, 1)),
        )

    def push_strip(member, value, ok):
        move = VEL[member]
        value = jnp.where(ok, value, ROCK)
        value = turn(value, move[0] * cols + move[2], 1)
        return turn(value, move[1], 0)

    from_low = lane % cols == HALO
    fills = {}
    for member in range(NP):
        if VEL[member][2] > 0:
            base = 0 if member < NF else NF
            move = VEL[member]
            twin = base + VEL_F.index((move[0], move[1], -1))
            fills[member] = fills[twin] = (len(fills) // 2, member, twin)

    def to_ends(values, at):
        return pltpu.roll(values, (2 * cz - (at * cols + HALO)) % cz, axis=1)

    def main_grads(source, fill, at):
        here = source[at]
        fill = to_ends(fill, at)
        down = jnp.where(lane == 0, fill, turn(here, 1, 1))
        up = jnp.where(lane == cz - 1, fill, turn(here, -1, 1))
        return (
            0.5 * (source[at + 1] - source[at - 1]),
            0.5 * (turn(here, -1, 0) - turn(here, 1, 0)),
            0.5 * (up - down),
        )

    def push_z(member, value, source, at, part, memo):
        move = VEL[member]
        if move[2] == 0:
            return value
        size = value.shape[0]
        number = fills[member][0]
        if number not in memo:
            memo[number] = to_ends(source[number, part], at + move[0])
        edge = 0 if move[2] > 0 else cz - 1
        return jnp.where(lane[:size] == edge, memo[number], turn(value, move[2], 1))

    def push_main(member, value, ok, at, memo):
        value = turn(jnp.where(ok, value, ROCK), VEL[member][1], 0)
        return push_z(member, value, fill_moved, at, pl.ds(0, rows), memo)

    totals = []
    for side in range(2):
        ok = strip_fluid[side] == 1.0
        values = [strip_pops[side, member] for member in range(NP)]
        total = jnp.where(ok, add_up(values[NF:]), 0.0)
        totals.append(turn(total, 1 if side == 0 else -1, 1))
        done = relax_rest(total, strip_grads(total), dict(enumerate(values)))
        for member in range(NP):
            strip_stayed[side, member] = done[member]
            strip_moved[side, member] = push_strip(member, done[member], ok)

    fill_phase = jnp.where(from_low, totals[0], totals[1])
    for number, low, high in sorted(set(fills.values())):
        fill_moved[number] = jnp.where(from_low, strip_moved[0, low], strip_moved[1, high])

    def collide(at, values):
        ok = fluid[at] == 1.0
        grads = main_grads(potential, fill_phase, at)
        done = relax_rest(potential[at], grads, dict(enumerate(values)))
        memo = {}
        for member in range(NP):
            stayed[member, at] = done[member]
            moved[member, at] = push_main(member, done[member], ok, at, memo)

    def collide_own(x, carry):
        collide(first + x, [whole(cells, cells_y, member, x) for member in range(NP)])
        return carry

    lax.fori_loop(0, cx, collide_own, 0, unroll=True)
    for end in ends:
        collide(
            jnp.where(end[2] == 0, first - 1, last + 1),
            [whole_face(end, member) for member in range(NP)],
        )
    for side in range(2):
        at = at_depth(side, 2)
        members = {m + side: face[side, L_F2 + slot] for slot, m in enumerate(IN_F)}
        members.update({NF + m: face[side, L_G2 + m] for m in range(NG)})
        done = relax_rest(potential[at], main_grads(potential, fill_phase, at), members)
        ok = fluid[at] == 1.0
        memo = {}
        for member in done:
            stayed[member, at] = done[member]
            moved[member, at] = push_main(member, done[member], ok, at, memo)
        at = at_depth(side, 3)
        member = NF + IN_G + side
        done = relax_rest(
            potential[at], main_grads(potential, fill_phase, at), {member: face[side, L_G3]}
        )
        ok = fluid[at] == 1.0
        moved[member, at] = push_main(member, done[member], ok, at, {})

    def pull(member, at, part):
        if VEL[member] == (0, 0, 0):
            return stayed[member, at, part]
        value = moved[member, at - VEL[member][0], part]
        return jnp.where(value == ROCK, stayed[OPP[member], at, part], value)

    def stream(j, carry):
        at = first - 2 + j
        values = [pull(NF + member, at, pl.ds(0, rows)) for member in range(NG)]
        for member in range(NG):
            phase_pops[member, at] = values[member]
        potential1[at] = jnp.where(fluid[at] == 1.0, add_up(values), 0.0)
        return carry

    lax.fori_loop(0, cx + 4, stream, 0, unroll=True)

    totals = []
    crossed = {}
    for side in range(2):
        ok = strip_fluid[side] == 1.0
        values = []
        for member in range(NP):
            value = strip_moved[side, member]
            back = strip_stayed[side, OPP[member]]
            values.append(jnp.where(value == ROCK, back, value))
        total = jnp.where(ok, add_up(values[NF:]), 0.0)
        rho, mom = moments(values)
        sign = 1 if side == 0 else -1
        wanted = {m: values[m] for m in range(NP) if VEL[m][2] == sign}
        done = relax(rho, mom, total, strip_grads(total), wanted)
        for member in wanted:
            crossed[member] = push_strip(member, done[member], ok)
        totals.append(turn(total, sign, 1))
    fill_phase1 = jnp.where(from_low, totals[0], totals[1])
    for number, low, high in sorted(set(fills.values())):
        fill_moved1[number] = jnp.where(from_low, crossed[low], crossed[high])

    def collide1(at, wanted, keep):
        grads = main_grads(potential1, fill_phase1, at)
        halves = []
        for half in range(2):
            part = pl.ds(half * cy, cy)
            values = [pull(member, at, part) for member in range(NF)]
            values += [phase_pops[member, at, part] for member in range(NG)]
            rho, mom = moments(values)
            members = [m for m in wanted if half == 0 or VEL[m][1] != 0]
            done = relax(
                rho, mom, potential1[at, part],
                [g[half * cy : (half + 1) * cy] for g in grads],
                {m: values[m] for m in members},
            )
            halves.append((done, fluid[at, part] == 1.0))
        (done, ok), (done_y, ok_y) = halves
        memo = {}
        for member in wanted:
            if keep:
                stayed1[member, at] = done[member]
            step_y = VEL[member][1]
            value = turn(jnp.where(ok, done[member], ROCK), step_y, 0)
            if step_y:
                value_y = turn(jnp.where(ok_y, done_y[member], ROCK), step_y, 0)
                edge = 0 if step_y > 0 else cy - 1
                value = jnp.where(row[:cy] == edge, value_y, value)
            moved1[member, at] = push_z(member, value, fill_moved1, at, own_rows, memo)

    def outputs(x):
        return (
            pltpu.make_async_copy(
                result.at[pl.ds(0, NF), x], flow_out.at[:, x], sem.at[0, x]
            ),
            pltpu.make_async_copy(
                result.at[pl.ds(NF, NG), x], phase_out.at[:, x], sem.at[1, x]
            ),
        )

    def finish(x):
        at = first + x
        ok = fluid[at, own_rows] == 1.0
        for member in range(NP):
            if VEL[member] == (0, 0, 0):
                value = stayed1[member, at]
            else:
                value = moved1[member, at - VEL[member][0]]
                value = jnp.where(value == ROCK, stayed1[OPP[member], at], value)
            result[member, x] = jnp.where(ok, value, own[member, x])
        for one in outputs(x):
            one.start()

    collide1(first - 1, [m for m in range(NP) if VEL[m][0] == 1], False)
    for x in range(cx):
        collide1(first + x, range(NP), True)
        if x > 0:
            finish(x - 1)
    collide1(last + 1, [m for m in range(NP) if VEL[m][0] == -1], False)
    finish(cx - 1)
    for x in range(cx):
        for one in outputs(x):
            one.wait()


def shards(sizes, flow_pops, phase_pops, pore_mask):
    cx, cy, cz = pore_mask.shape
    rows = 2 * cy
    assert cx >= HALO and cy == 2 * HALO and 6 * cx * HALO <= cz
    f32 = jnp.float32
    vmem = pl.BlockSpec(memory_space=pltpu.VMEM)
    anywhere = pl.BlockSpec(memory_space=pl.ANY)

    def near(*arrays):
        return [pltpu.with_memory_space_constraint(a, pltpu.VMEM) for a in arrays]

    def call(kernel, out_shape, in_specs, args, scratch=(), out_specs=None):
        return pl.pallas_call(
            kernel,
            out_shape=out_shape,
            in_specs=in_specs,
            out_specs=out_specs or jax.tree.map(lambda _: vmem, out_shape),
            scratch_shapes=scratch,
        )(*args)

    end_blocks = pl.cdiv(NV, cz // (2 * HALO * cx))
    end_shape = pltpu.VMEM((end_blocks, cy, cz), f32)
    z_shape = pltpu.VMEM((pl.cdiv(end_blocks, 2), cy, cz), f32)
    own, cells, ends, z_a, z_b = call(
        load_kernel,
        (
            pltpu.VMEM((NP, cx, cy, cz), f32),
            pltpu.VMEM((NV, cx, cy, cz), f32),
            end_shape,
            z_shape,
            z_shape,
        ),
        [anywhere] * 3, (flow_pops, phase_pops, pore_mask),
        [
            pltpu.VMEM(pore_mask.shape, jnp.int32),
            pltpu.SemaphoreType.DMA((3,)),
        ],
    )
    cells_y = beside(sizes, cells)
    z_a, z_b = swap(sizes, "gz", z_a, z_b)

    x_shape = pltpu.VMEM((NV + N_FACE, cy, cz), f32)
    x_a, x_b = call(faces_kernel, (x_shape, x_shape), [vmem], near(cells))
    x_a, x_b = swap(sizes, "gx", x_a, x_b)
    x_a_y = beside(sizes, x_a)
    x_b_y = beside(sizes, x_b)

    strip_blocks = 2 * end_blocks
    strips = call(
        lambda *refs: strips_kernel(*refs, sizes=sizes),
        pltpu.VMEM((strip_blocks, cy, cz), f32), [vmem] * 3, near(ends, z_a, z_b),
    )
    strips_y = beside(sizes, strips)
    far_a, far_b = swap(sizes, "gx", strips, strips)
    far_a_y = beside(sizes, far_a)
    far_b_y = beside(sizes, far_b)

    deep = cx + 2 * HALO

    def block(*lead):
        return pltpu.VMEM((*lead, rows, cz), f32)

    return call(
        lambda *refs: steps_kernel(*refs, sizes=sizes),
        (
            jax.ShapeDtypeStruct(flow_pops.shape, f32),
            jax.ShapeDtypeStruct(phase_pops.shape, f32),
        ),
        [vmem] * 13,
        near(
            own, cells, cells_y, strips, strips_y, far_a, far_b, far_a_y, far_b_y,
            x_a, x_b, x_a_y, x_b_y,
        ),
        [
            block(2, N_FACE),
            block(deep),
            block(deep),
            block(2, NP),
            block(2),
            block(6),
            block(6),
            block(NP, deep),
            block(NP, deep),
            block(2, NP),
            block(2, NP),
            block(NG, deep),
            block(deep),
            pltpu.VMEM((NP, deep, cy, cz), f32),
            pltpu.VMEM((NP, deep, cy, cz), f32),
            pltpu.VMEM((NP, cx, cy, cz), f32),
            pltpu.SemaphoreType.DMA((2, cx)),
        ],
        (anywhere, anywhere),
    )


def solution(mesh):
    sizes = dict(mesh.shape)
    placed = (P(None, "gx", "gy", "gz"), P(None, "gx", "gy", "gz"), P("gx", "gy", "gz"))
    return jax.shard_map(
        lambda *args: shards(sizes, *args),
        mesh=mesh,
        in_specs=placed,
        out_specs=(P(None, "gx", "gy", "gz"), P(None, "gx", "gy", "gz")),
        check_vma=False,
    )
```

```python
import jax
import jax.numpy as jnp
from jax import lax
from jax.experimental import pallas as pl
from jax.experimental.pallas import tpu as pltpu
from jax.sharding import PartitionSpec as P


AXES = ("gx", "gy", "gz")

VEL_F = [
    (0, 0, 0),
    (1, 0, 0),
    (-1, 0, 0),
    (0, 1, 0),
    (0, -1, 0),
    (0, 0, 1),
    (0, 0, -1),
    (1, 1, 0),
    (-1, -1, 0),
    (1, -1, 0),
    (-1, 1, 0),
    (1, 0, 1),
    (-1, 0, -1),
    (1, 0, -1),
    (-1, 0, 1),
    (0, 1, 1),
    (0, -1, -1),
    (0, 1, -1),
    (0, -1, 1),
]
OPP_F = [0, 2, 1, 4, 3, 6, 5, 8, 7, 10, 9, 12, 11, 14, 13, 16, 15, 18, 17]
NF = 19
NG = 7
NP = NF + NG
VEL = VEL_F + VEL_F[:NG]
OPP = OPP_F + [NF + other for other in OPP_F[:NG]]

HALO = 4
ROCK = 3.0e38

IN_F = [1, 7, 9, 11, 13]
IN_G = 1
NV = NP + 1
L_G2 = 0
L_F2 = L_G2 + NG
L_G3 = L_F2 + len(IN_F)
L_PH3 = L_G3 + 1
L_PH4 = L_PH3 + 1
L_MASK = L_PH4 + 1
N_FACE = L_MASK + 2


def pairing(sizes, axis, first):
    spare = "gy" if axis != "gy" else "gx"
    perm = []
    real = False

    def linear(at):
        return (at["gx"] * sizes["gy"] + at["gy"]) * sizes["gz"] + at["gz"]

    for gx in range(sizes["gx"]):
        for gy in range(sizes["gy"]):
            for gz in range(sizes["gz"]):
                at = {"gx": gx, "gy": gy, "gz": gz}
                other = at[axis] + (1 if at[axis] % 2 == first else -1)
                if 0 <= other < sizes[axis]:
                    real = True
                    perm.append((linear(at), linear({**at, axis: other})))
                elif at[spare] ^ 1 < sizes[spare]:
                    perm.append((linear(at), linear({**at, spare: at[spare] ^ 1})))
    return perm if real else None


def swap(sizes, axis, send_a, send_b):
    perm_a = pairing(sizes, axis, 0)
    perm_b = pairing(sizes, axis, 1)
    got_a = lax.ppermute(send_a, AXES, perm_a) if perm_a else send_a
    got_b = lax.ppermute(send_b, AXES, perm_b) if perm_b else got_a
    return got_a, got_b


def beside(sizes, cells):
    if sizes["gy"] <= 2:
        perm = pairing(sizes, "gy", 0)
        return lax.ppermute(cells, AXES, perm) if perm else cells
    got_a, got_b = swap(sizes, "gy", cells, cells)
    even = lax.axis_index("gy") % 2 == 0
    above = jnp.where(even, got_a, got_b)
    below = jnp.where(even, got_b, got_a)
    row = lax.broadcasted_iota(jnp.int32, cells.shape, cells.ndim - 2)
    return jnp.where(row < HALO, above, below)


def relax(rho, mom, phase, grads, pops):
    inv = 1.0 / rho
    vel = [m * inv for m in mom]
    if grads is not None:
        square = grads[0] * grads[0] + grads[1] * grads[1] + grads[2] * grads[2] + 0.01
        inv_mag = lax.rsqrt(square)
        mag = square * inv_mag
    out = {}
    if any(member < NF for member in pops):
        omega = 1.0 / (0.8 + 0.2 * phase)
        keep = 1.0 - omega
        scale = omega * rho
        base = scale * (1.0 - 1.5 * (vel[0] * vel[0] + vel[1] * vel[1] + vel[2] * vel[2]))
        quad_v = [4.5 * scale * v for v in vel]
        lin = [(3.0 * scale) * v for v in vel]
        diag = [quad_v[d] * vel[d] for d in range(3)]
        tail = {0: 0.0, 1: 0.0, 2: 0.0}
        if grads is not None:
            quad_g = [0.5 * inv_mag * g for g in grads]
            diag = [diag[d] + quad_g[d] * grads[d] for d in range(3)]
            tail = {
                0: (1.0 / 9.0) * mag,
                1: (-0.5 / 54.0) * mag,
                2: (-0.5 / 27.0) * mag,
            }

        def cross(a, b):
            total = quad_v[a] * vel[b]
            if grads is not None:
                total = total + quad_g[a] * grads[b]
            return 2.0 * total

        memo = {}

        def once(key, make):
            if key not in memo:
                memo[key] = make()
            return memo[key]

        for member in pops:
            if member >= NF:
                continue
            dims = [d for d in range(3) if VEL[member][d] != 0]
            signs = [VEL[member][d] for d in dims]
            if not dims:
                out[member] = keep * pops[member] + ((1.0 / 3.0) * base + tail[0])
                continue
            if len(dims) == 1:
                d = dims[0]
                even = once(("e", d), lambda: (1.0 / 18.0) * (base + diag[d]) + tail[1])
                odd = once(("o", d), lambda: (1.0 / 18.0) * lin[d])
                flip = signs[0]
            else:
                a, b = dims
                same = signs[0] * signs[1]
                both = once(("s", a, b), lambda: base + diag[a] + diag[b])
                mixed = once(("m", a, b), lambda: cross(a, b))
                even = once(
                    ("e", a, b, same),
                    lambda: (1.0 / 36.0) * (both + mixed if same > 0 else both - mixed) + tail[2],
                )
                odd = once(
                    ("o", a, b, same),
                    lambda: (1.0 / 36.0) * (lin[a] + lin[b] if same > 0 else lin[a] - lin[b]),
                )
                flip = signs[0]
            mid = keep * pops[member] + even
            out[member] = mid + odd if flip > 0 else mid - odd
    if any(member >= NF for member in pops):
        part = 1.25 * 0.125
        if grads is not None:
            sharpen = 0.7 * (1.0 - phase * phase) * inv_mag
        for member in pops:
            if member < NF:
                continue
            move = VEL[member]
            if move == (0, 0, 0):
                out[member] = (1.25 * 0.25) * phase - 0.25 * pops[member]
                continue
            d = [i for i in range(3) if move[i] != 0][0]
            drift = 4.0 * phase * vel[d]
            if grads is not None:
                drift = drift + sharpen * grads[d]
            still = part * phase - 0.25 * pops[member]
            out[member] = still + part * drift if move[d] > 0 else still - part * drift
    return out


def relax_rest(phase, grads, pops):
    square = grads[0] * grads[0] + grads[1] * grads[1] + grads[2] * grads[2] + 0.01
    inv_mag = lax.rsqrt(square)
    mag = square * inv_mag
    half = 0.5 * inv_mag
    sharpen = (1.25 * 0.125 * 0.7) * (1.0 - phase * phase) * inv_mag
    quad = [half * g for g in grads]
    diag = [quad[d] * grads[d] for d in range(3)]
    memo = {}
    out = {}
    for member in pops:
        move = VEL[member]
        dims = [d for d in range(3) if move[d] != 0]
        if member >= NF:
            if dims:
                d = dims[0]
                if d not in memo:
                    memo[d] = sharpen * grads[d]
                out[member] = pops[member] + memo[d] if move[d] > 0 else pops[member] - memo[d]
            else:
                out[member] = pops[member]
            continue
        key = tuple(abs(v) for v in move) + (
            (move[dims[0]] * move[dims[1]],) if len(dims) == 2 else ()
        )
        if key not in memo:
            if not dims:
                memo[key] = (1.0 / 9.0) * mag
            elif len(dims) == 1:
                memo[key] = (1.0 / 18.0) * diag[dims[0]] - (0.5 / 54.0) * mag
            else:
                a, b = dims
                mixed = 2.0 * (quad[a] * grads[b])
                both = diag[a] + diag[b]
                both = both + mixed if key[3] > 0 else both - mixed
                memo[key] = (1.0 / 36.0) * both - (0.5 / 27.0) * mag
        out[member] = pops[member] + memo[key]
    return out


def moments(pops):
    rho = pops[0]
    for member in range(1, NF):
        rho = rho + pops[member]
    mom = []
    for d in range(3):
        plus = [pops[m] for m in range(NF) if VEL[m][d] > 0]
        minus = [pops[m] for m in range(NF) if VEL[m][d] < 0]
        total = plus[0] - minus[0]
        for p, m in zip(plus[1:], minus[1:]):
            total = total + (p - m)
        mom.append(total)
    return rho, mom


def add_up(values):
    total = values[0]
    for value in values[1:]:
        total = total + value
    return total


def turn(value, shift, dim):
    size = value.shape[dim]
    shift = shift % size
    return pltpu.roll(value, shift, axis=dim) if shift else value


def load_kernel(flow, phase, mask, own, cells, ends, out_a, out_b, mask_in, sem):
    _, cx, cy, cz = own.shape
    copies = [
        pltpu.make_async_copy(flow, own.at[pl.ds(0, NF)], sem.at[0]),
        pltpu.make_async_copy(phase, own.at[pl.ds(NF, NG)], sem.at[1]),
        pltpu.make_async_copy(mask, mask_in, sem.at[2]),
    ]
    for one in copies:
        one.start()
    for one in copies:
        one.wait()
    cells[NP] = mask_in[...].astype(jnp.float32)
    for x in range(cx):
        values = [own[member, x] for member in range(NP)]
        rho, mom = moments(values)
        done = relax(rho, mom, add_up(values[NF:]), None, dict(enumerate(values)))
        for member in range(NP):
            cells[member, x] = done[member]
    even = lax.axis_index("gz") % 2 == 0
    lane = lax.broadcasted_iota(jnp.int32, (cy, cz), 1)
    group = lane // (2 * HALO)
    first_half = lane % (2 * HALO) < HALO
    per = cz // (2 * HALO * cx)
    for block in range(ends.shape[0]):
        total = jnp.zeros((cy, cz), jnp.float32)
        for field in range(block * per, min((block + 1) * per, NV)):
            for x in range(cx):
                slot = (field % per) * cx + x
                value = turn(cells[field, x], slot * 2 * HALO + HALO, 1)
                total = jnp.where(group == slot, value, total)
        ends[block] = total
    for pair in range(out_a.shape[0]):
        one = ends[2 * pair]
        two = ends[min(2 * pair + 1, ends.shape[0] - 1)]
        high = jnp.where(first_half, one, turn(two, HALO, 1))
        low = jnp.where(first_half, turn(one, -HALO, 1), two)
        out_a[pair] = jnp.where(even, high, low)
        out_b[pair] = jnp.where(even, low, high)


def pack_face(own, out, base, up):
    cx = own.shape[1]
    other = jnp.where(up, 0, 1)
    xs = [jnp.where(up, cx - 1 - d, d) for d in range(HALO)]
    for field in range(NV):
        out[base + field] = own[field, xs[0]]
    base = base + NV
    for member in range(NG):
        out[base + L_G2 + member] = own[NF + member, xs[1]]
    for slot, member in enumerate(IN_F):
        out[base + L_F2 + slot] = own[member + other, xs[1]]
    out[base + L_G3] = own[NF + IN_G + other, xs[2]]
    out[base + L_PH3] = add_up([own[NF + member, xs[2]] for member in range(NG)])
    far = add_up([own[NF + member, xs[3]] for member in range(NG)])
    out[base + L_PH4] = jnp.where(own[NP, xs[3]] == 1.0, far, 0.0)
    for d in range(2):
        out[base + L_MASK + d] = own[NP, xs[1 + d]]


def faces_kernel(own, out_a, out_b):
    even = lax.axis_index("gx") % 2 == 0
    pack_face(own, out_a, 0, even)
    pack_face(own, out_b, 0, jnp.logical_not(even))


def merged(cx, cz):
    return NF // (cz // (2 * HALO * cx)) // 2


def strips_kernel(ends, z_a, z_b, strips, out_a, out_b, *, sizes, cx):
    blocks, cy, cz = ends.shape
    at_z = lax.axis_index("gz")
    even = at_z % 2 == 0
    lane = lax.broadcasted_iota(jnp.int32, (cy, cz), 1)
    first_half = lane % (2 * HALO) < HALO
    has_below = at_z > 0
    has_above = at_z < sizes["gz"] - 1
    for block in range(blocks):
        from_a, from_b = z_a[block // 2], z_b[block // 2]
        below = jnp.where(even, from_b, from_a)
        above = jnp.where(even, from_a, from_b)
        if block % 2 == 0:
            above = turn(above, HALO, 1)
        else:
            below = turn(below, -HALO, 1)
        if block == blocks - 1:
            below = jnp.where(has_below, below, 0.0)
            above = jnp.where(has_above, above, 0.0)
        own = ends[block]
        strips[block] = jnp.where(first_half, below, own)
        strips[blocks + block] = jnp.where(first_half, own, above)

    wide = 2 * HALO * cx
    pairs = merged(cx, cz)
    even_x = lax.axis_index("gx") % 2 == 0
    count = out_a.shape[0] // 2
    upper = lane % wide >= wide // 2
    for out, up in ((out_a, even_x), (out_b, jnp.logical_not(even_x))):
        near = upper == up
        shift = jnp.where(up, cz - wide // 2, wide // 2)
        for side in range(2):
            for pair in range(pairs):
                one = strips[side * blocks + 2 * pair]
                two = pltpu.roll(strips[side * blocks + 2 * pair + 1], shift, axis=1)
                out[side * count + pair] = jnp.where(near, one, two)
            for block in range(2 * pairs, blocks):
                out[side * count + block - pairs] = strips[side * blocks + block]


def steps_kernel(
    own, cells, cells_y, strips, strips_y, far_a, far_b, far_a_y, far_b_y,
    x_a, x_b, x_a_y, x_b_y,
    flow_out, phase_out,
    face, fluid, potential,
    strip_pops, strip_fluid, fill_moved, fill_moved1, moved, stayed, strip_moved, strip_stayed,
    phase_pops, potential1, moved1, stayed1, result, sem,
    *, sizes,
):
    _, cx, cy, cz = own.shape
    rows = 2 * cy
    at_x = lax.axis_index("gx")
    at_y = lax.axis_index("gy")
    even_x = at_x % 2 == 0
    first, last = HALO, HALO + cx - 1
    own_rows = pl.ds(0, cy)

    def whole(cells, cells_y, *at):
        return jnp.concatenate([cells[at], cells_y[at]], axis=0)

    lane = lax.broadcasted_iota(jnp.int32, (rows, cz), 1)
    row = lax.broadcasted_iota(jnp.int32, (rows, cz), 0)
    has_left = at_x > 0
    has_right = at_x < sizes["gx"] - 1
    has_low = at_y > 0
    has_high = at_y < sizes["gy"] - 1
    high_row = jnp.where(has_high, cy + HALO, cy)
    low_row = jnp.where(has_low, cy + HALO, rows)
    row_ok = (row < high_row) | (row >= low_row)
    has = (has_left, has_right)

    def at_depth(side, depth):
        return first - depth if side == 0 else last + depth

    side_a = jnp.where(even_x, 1, 0)
    ends = ((x_a, x_a_y, side_a), (x_b, x_b_y, 1 - side_a))

    def whole_face(end, layer):
        return whole(end[0], end[1], layer)

    for x in range(cx):
        ok = (whole(cells, cells_y, NP, x) == 1.0) & row_ok
        fluid[first + x] = ok.astype(jnp.float32)
        total = add_up([whole(cells, cells_y, NF + member, x) for member in range(NG)])
        potential[first + x] = jnp.where(ok, total, 0.0)
    for end in ends:
        side = end[2]
        for layer in range(N_FACE):
            face[side, layer] = whole_face(end, NV + layer)
        at = jnp.where(side == 0, first - 1, last + 1)
        side_ok = row_ok & ((side == 0) & has_left | (side == 1) & has_right)
        ok = side_ok & (whole_face(end, NP) == 1.0)
        total = add_up([whole_face(end, NF + member) for member in range(NG)])
        fluid[at] = ok.astype(jnp.float32)
        potential[at] = jnp.where(ok, total, 0.0)
    for side in range(2):
        side_ok = row_ok & has[side]
        for depth in range(2, HALO + 1):
            at = at_depth(side, depth)
            ok = side_ok
            if depth == 2:
                total = add_up([face[side, L_G2 + m] for m in range(NG)])
            else:
                total = face[side, L_PH3 if depth == 3 else L_PH4]
            if depth < HALO:
                ok = ok & (face[side, L_MASK + depth - 2] == 1.0)
                fluid[at] = ok.astype(jnp.float32)
            potential[at] = jnp.where(ok, total, 0.0)

    cols = 2 * HALO
    wide = cols * cx
    per = cz // wide
    block_ok = row_ok & (
        ((lane < wide) & has_left)
        | ((lane >= wide) & (lane < 2 * wide))
        | ((lane >= 2 * wide) & (lane < 3 * wide) & has_right)
    )
    blocks = strips.shape[0] // 2
    count = far_a.shape[0] // 2
    pairs = merged(cx, cz)
    group = lane // wide
    for side in range(2):
        for block in range(blocks):
            second = block < 2 * pairs and block % 2
            at = side * count + (block // 2 if block < 2 * pairs else block - pairs)
            from_a = whole(far_a, far_a_y, at)
            from_b = whole(far_b, far_b_y, at)
            left = jnp.where(even_x, from_b, from_a)
            right = jnp.where(even_x, from_a, from_b)
            left = turn(left, wide // 2 if second else 0, 1)
            right = turn(right, 2 * wide - (wide // 2 if second else 0), 1)
            mine = turn(whole(strips, strips_y, side * blocks + block), wide, 1)
            for field in range(block * per, min((block + 1) * per, NV)):
                spot = field % per
                value = jnp.where(
                    group == spot, left, jnp.where(group == (spot + 1) % per, mine, right)
                )
                value = turn(value, -spot * wide, 1)
                if field < NP:
                    strip_pops[side, field] = value
                else:
                    strip_fluid[side] = jnp.where(block_ok, value, 0.0)

    def strip_grads(values):
        return (
            0.5 * (turn(values, -cols, 1) - turn(values, cols, 1)),
            0.5 * (turn(values, -1, 0) - turn(values, 1, 0)),
            0.5 * (turn(values, -1, 1) - turn(values, 1, 1)),
        )

    def push_strip(member, value, ok):
        move = VEL[member]
        value = jnp.where(ok, value, ROCK)
        value = turn(value, move[0] * cols + move[2], 1)
        return turn(value, move[1], 0)

    from_low = lane % cols == HALO
    fills = {}
    for member in range(NP):
        if VEL[member][2] > 0:
            base = 0 if member < NF else NF
            move = VEL[member]
            twin = base + VEL_F.index((move[0], move[1], -1))
            fills[member] = fills[twin] = (len(fills) // 2, member, twin)

    def to_ends(values, at):
        return pltpu.roll(values, (2 * cz - (at * cols + HALO)) % cz, axis=1)

    def main_grads(source, fill, at):
        here = source[at]
        fill = to_ends(fill, at)
        down = jnp.where(lane == 0, fill, turn(here, 1, 1))
        up = jnp.where(lane == cz - 1, fill, turn(here, -1, 1))
        return (
            0.5 * (source[at + 1] - source[at - 1]),
            0.5 * (turn(here, -1, 0) - turn(here, 1, 0)),
            0.5 * (up - down),
        )

    def push_z(member, value, source, at, part, memo):
        move = VEL[member]
        if move[2] == 0:
            return value
        size = value.shape[0]
        number = fills[member][0]
        if number not in memo:
            memo[number] = to_ends(source[number, part], at + move[0])
        edge = 0 if move[2] > 0 else cz - 1
        return jnp.where(lane[:size] == edge, memo[number], turn(value, move[2], 1))

    def push_main(member, value, ok, at, memo):
        value = turn(jnp.where(ok, value, ROCK), VEL[member][1], 0)
        return push_z(member, value, fill_moved, at, pl.ds(0, rows), memo)

    totals = []
    for side in range(2):
        ok = strip_fluid[side] == 1.0
        values = [strip_pops[side, member] for member in range(NP)]
        total = jnp.where(ok, add_up(values[NF:]), 0.0)
        totals.append(turn(total, 1 if side == 0 else -1, 1))
        done = relax_rest(total, strip_grads(total), dict(enumerate(values)))
        for member in range(NP):
            strip_stayed[side, member] = done[member]
            strip_moved[side, member] = push_strip(member, done[member], ok)

    fill_phase = jnp.where(from_low, totals[0], totals[1])
    for number, low, high in sorted(set(fills.values())):
        fill_moved[number] = jnp.where(from_low, strip_moved[0, low], strip_moved[1, high])

    def collide(at, values):
        ok = fluid[at] == 1.0
        grads = main_grads(potential, fill_phase, at)
        done = relax_rest(potential[at], grads, dict(enumerate(values)))
        memo = {}
        for member in range(NP):
            stayed[member, at] = done[member]
            moved[member, at] = push_main(member, done[member], ok, at, memo)

    def collide_own(x, carry):
        collide(first + x, [whole(cells, cells_y, member, x) for member in range(NP)])
        return carry

    lax.fori_loop(0, cx, collide_own, 0, unroll=2)
    for end in ends:
        collide(
            jnp.where(end[2] == 0, first - 1, last + 1),
            [whole_face(end, member) for member in range(NP)],
        )
    for side in range(2):
        at = at_depth(side, 2)
        members = {m + side: face[side, L_F2 + slot] for slot, m in enumerate(IN_F)}
        members.update({NF + m: face[side, L_G2 + m] for m in range(NG)})
        done = relax_rest(potential[at], main_grads(potential, fill_phase, at), members)
        ok = fluid[at] == 1.0
        memo = {}
        for member in done:
            stayed[member, at] = done[member]
            moved[member, at] = push_main(member, done[member], ok, at, memo)
        at = at_depth(side, 3)
        member = NF + IN_G + side
        done = relax_rest(
            potential[at], main_grads(potential, fill_phase, at), {member: face[side, L_G3]}
        )
        ok = fluid[at] == 1.0
        moved[member, at] = push_main(member, done[member], ok, at, {})

    def pull(member, at, part):
        if VEL[member] == (0, 0, 0):
            return stayed[member, at, part]
        value = moved[member, at - VEL[member][0], part]
        return jnp.where(value == ROCK, stayed[OPP[member], at, part], value)

    def stream(j, carry):
        at = first - 2 + j
        values = [pull(NF + member, at, pl.ds(0, rows)) for member in range(NG)]
        for member in range(NG):
            phase_pops[member, at] = values[member]
        potential1[at] = jnp.where(fluid[at] == 1.0, add_up(values), 0.0)
        return carry

    lax.fori_loop(0, cx + 4, stream, 0, unroll=2)

    totals = []
    crossed = {}
    for side in range(2):
        ok = strip_fluid[side] == 1.0
        values = []
        for member in range(NP):
            value = strip_moved[side, member]
            back = strip_stayed[side, OPP[member]]
            values.append(jnp.where(value == ROCK, back, value))
        total = jnp.where(ok, add_up(values[NF:]), 0.0)
        rho, mom = moments(values)
        sign = 1 if side == 0 else -1
        wanted = {m: values[m] for m in range(NP) if VEL[m][2] == sign}
        done = relax(rho, mom, total, strip_grads(total), wanted)
        for member in wanted:
            crossed[member] = push_strip(member, done[member], ok)
        totals.append(turn(total, sign, 1))
    fill_phase1 = jnp.where(from_low, totals[0], totals[1])
    for number, low, high in sorted(set(fills.values())):
        fill_moved1[number] = jnp.where(from_low, crossed[low], crossed[high])

    def collide1(at, wanted, keep):
        grads = main_grads(potential1, fill_phase1, at)
        halves = []
        for half in range(2):
            part = pl.ds(half * cy, cy)
            values = [pull(member, at, part) for member in range(NF)]
            values += [phase_pops[member, at, part] for member in range(NG)]
            rho, mom = moments(values)
            members = [m for m in wanted if half == 0 or VEL[m][1] != 0]
            done = relax(
                rho, mom, potential1[at, part],
                [g[half * cy : (half + 1) * cy] for g in grads],
                {m: values[m] for m in members},
            )
            halves.append((done, fluid[at, part] == 1.0))
        (done, ok), (done_y, ok_y) = halves
        memo = {}
        for member in wanted:
            if keep:
                stayed1[member, at] = done[member]
            step_y = VEL[member][1]
            value = turn(jnp.where(ok, done[member], ROCK), step_y, 0)
            if step_y:
                value_y = turn(jnp.where(ok_y, done_y[member], ROCK), step_y, 0)
                edge = 0 if step_y > 0 else cy - 1
                value = jnp.where(row[:cy] == edge, value_y, value)
            moved1[member, at] = push_z(member, value, fill_moved1, at, own_rows, memo)

    def outputs(x):
        return (
            pltpu.make_async_copy(
                result.at[pl.ds(0, NF), x], flow_out.at[:, x], sem.at[0, x]
            ),
            pltpu.make_async_copy(
                result.at[pl.ds(NF, NG), x], phase_out.at[:, x], sem.at[1, x]
            ),
        )

    def finish(x):
        at = first + x
        ok = fluid[at, own_rows] == 1.0
        for member in range(NP):
            if VEL[member] == (0, 0, 0):
                value = stayed1[member, at]
            else:
                value = moved1[member, at - VEL[member][0]]
                value = jnp.where(value == ROCK, stayed1[OPP[member], at], value)
            result[member, x] = jnp.where(ok, value, own[member, x])
        for one in outputs(x):
            one.start()

    collide1(first - 1, [m for m in range(NP) if VEL[m][0] == 1], False)
    for x in range(cx):
        collide1(first + x, range(NP), True)
        if x > 0:
            finish(x - 1)
    collide1(last + 1, [m for m in range(NP) if VEL[m][0] == -1], False)
    finish(cx - 1)
    for x in range(cx):
        for one in outputs(x):
            one.wait()


def shards(sizes, flow_pops, phase_pops, pore_mask):
    cx, cy, cz = pore_mask.shape
    rows = 2 * cy
    assert cx >= HALO and cy == 2 * HALO and 6 * cx * HALO <= cz
    f32 = jnp.float32
    vmem = pl.BlockSpec(memory_space=pltpu.VMEM)
    anywhere = pl.BlockSpec(memory_space=pl.ANY)

    def near(*arrays):
        return [pltpu.with_memory_space_constraint(a, pltpu.VMEM) for a in arrays]

    def call(kernel, out_shape, in_specs, args, scratch=(), out_specs=None):
        return pl.pallas_call(
            kernel,
            out_shape=out_shape,
            in_specs=in_specs,
            out_specs=out_specs or jax.tree.map(lambda _: vmem, out_shape),
            scratch_shapes=scratch,
        )(*args)

    end_blocks = pl.cdiv(NV, cz // (2 * HALO * cx))
    end_shape = pltpu.VMEM((end_blocks, cy, cz), f32)
    z_shape = pltpu.VMEM((pl.cdiv(end_blocks, 2), cy, cz), f32)
    own, cells, ends, z_a, z_b = call(
        load_kernel,
        (
            pltpu.VMEM((NP, cx, cy, cz), f32),
            pltpu.VMEM((NV, cx, cy, cz), f32),
            end_shape,
            z_shape,
            z_shape,
        ),
        [anywhere] * 3, (flow_pops, phase_pops, pore_mask),
        [
            pltpu.VMEM(pore_mask.shape, jnp.int32),
            pltpu.SemaphoreType.DMA((3,)),
        ],
    )
    cells_y = beside(sizes, cells)
    z_a, z_b = swap(sizes, "gz", z_a, z_b)

    x_shape = pltpu.VMEM((NV + N_FACE, cy, cz), f32)
    x_a, x_b = call(faces_kernel, (x_shape, x_shape), [vmem], near(cells))
    x_a, x_b = swap(sizes, "gx", x_a, x_b)
    x_a_y = beside(sizes, x_a)
    x_b_y = beside(sizes, x_b)

    strip_blocks = 2 * end_blocks
    far_shape = pltpu.VMEM((strip_blocks - 2 * merged(cx, cz), cy, cz), f32)
    strips, far_a, far_b = call(
        lambda *refs: strips_kernel(*refs, sizes=sizes, cx=cx),
        (pltpu.VMEM((strip_blocks, cy, cz), f32), far_shape, far_shape),
        [vmem] * 3, near(ends, z_a, z_b),
    )
    strips_y = beside(sizes, strips)
    far_a, far_b = swap(sizes, "gx", far_a, far_b)
    far_a_y = beside(sizes, far_a)
    far_b_y = beside(sizes, far_b)

    deep = cx + 2 * HALO

    def block(*lead):
        return pltpu.VMEM((*lead, rows, cz), f32)

    return call(
        lambda *refs: steps_kernel(*refs, sizes=sizes),
        (
            jax.ShapeDtypeStruct(flow_pops.shape, f32),
            jax.ShapeDtypeStruct(phase_pops.shape, f32),
        ),
        [vmem] * 13,
        near(
            own, cells, cells_y, strips, strips_y, far_a, far_b, far_a_y, far_b_y,
            x_a, x_b, x_a_y, x_b_y,
        ),
        [
            block(2, N_FACE),
            block(deep),
            block(deep),
            block(2, NP),
            block(2),
            block(6),
            block(6),
            block(NP, deep),
            block(NP, deep),
            block(2, NP),
            block(2, NP),
            block(NG, deep),
            block(deep),
            pltpu.VMEM((NP, deep, cy, cz), f32),
            pltpu.VMEM((NP, deep, cy, cz), f32),
            pltpu.VMEM((NP, cx, cy, cz), f32),
            pltpu.SemaphoreType.DMA((2, cx)),
        ],
        (anywhere, anywhere),
    )


def solution(mesh):
    sizes = dict(mesh.shape)
    placed = (P(None, "gx", "gy", "gz"), P(None, "gx", "gy", "gz"), P("gx", "gy", "gz"))
    return jax.shard_map(
        lambda *args: shards(sizes, *args),
        mesh=mesh,
        in_specs=placed,
        out_specs=(P(None, "gx", "gy", "gz"), P(None, "gx", "gy", "gz")),
        check_vma=False,
    )
```

```python
import jax
import jax.numpy as jnp
from jax import lax
from jax.experimental import pallas as pl
from jax.experimental.pallas import tpu as pltpu
from jax.sharding import PartitionSpec as P


AXES = ("gx", "gy", "gz")

VEL_F = [
    (0, 0, 0),
    (1, 0, 0),
    (-1, 0, 0),
    (0, 1, 0),
    (0, -1, 0),
    (0, 0, 1),
    (0, 0, -1),
    (1, 1, 0),
    (-1, -1, 0),
    (1, -1, 0),
    (-1, 1, 0),
    (1, 0, 1),
    (-1, 0, -1),
    (1, 0, -1),
    (-1, 0, 1),
    (0, 1, 1),
    (0, -1, -1),
    (0, 1, -1),
    (0, -1, 1),
]
OPP_F = [0, 2, 1, 4, 3, 6, 5, 8, 7, 10, 9, 12, 11, 14, 13, 16, 15, 18, 17]
NF = 19
NG = 7
NP = NF + NG
VEL = VEL_F + VEL_F[:NG]
OPP = OPP_F + [NF + other for other in OPP_F[:NG]]

HALO = 4
ROCK = 3.0e38

IN_F = [1, 7, 9, 11, 13]
IN_G = 1
NV = NP + 1
L_G2 = 0
L_F2 = L_G2 + NG
L_G3 = L_F2 + len(IN_F)
L_PH3 = L_G3 + 1
L_PH4 = L_PH3 + 1
L_MASK = L_PH4 + 1
N_FACE = L_MASK + 2


def pairing(sizes, axis, first):
    spare = "gy" if axis != "gy" else "gx"
    perm = []
    real = False

    def linear(at):
        return (at["gx"] * sizes["gy"] + at["gy"]) * sizes["gz"] + at["gz"]

    for gx in range(sizes["gx"]):
        for gy in range(sizes["gy"]):
            for gz in range(sizes["gz"]):
                at = {"gx": gx, "gy": gy, "gz": gz}
                other = at[axis] + (1 if at[axis] % 2 == first else -1)
                if 0 <= other < sizes[axis]:
                    real = True
                    perm.append((linear(at), linear({**at, axis: other})))
                elif at[spare] ^ 1 < sizes[spare]:
                    perm.append((linear(at), linear({**at, spare: at[spare] ^ 1})))
    return perm if real else None


def swap(sizes, axis, send_a, send_b):
    perm_a = pairing(sizes, axis, 0)
    perm_b = pairing(sizes, axis, 1)
    got_a = lax.ppermute(send_a, AXES, perm_a) if perm_a else send_a
    got_b = lax.ppermute(send_b, AXES, perm_b) if perm_b else got_a
    return got_a, got_b


def beside(sizes, cells):
    if sizes["gy"] <= 2:
        perm = pairing(sizes, "gy", 0)
        return lax.ppermute(cells, AXES, perm) if perm else cells
    got_a, got_b = swap(sizes, "gy", cells, cells)
    even = lax.axis_index("gy") % 2 == 0
    above = jnp.where(even, got_a, got_b)
    below = jnp.where(even, got_b, got_a)
    row = lax.broadcasted_iota(jnp.int32, cells.shape, cells.ndim - 2)
    return jnp.where(row < HALO, above, below)


def relax(rho, mom, phase, grads, pops):
    inv = 1.0 / rho
    vel = [m * inv for m in mom]
    if grads is not None:
        square = grads[0] * grads[0] + grads[1] * grads[1] + grads[2] * grads[2] + 0.01
        inv_mag = lax.rsqrt(square)
        mag = square * inv_mag
    out = {}
    if any(member < NF for member in pops):
        omega = 1.0 / (0.8 + 0.2 * phase)
        keep = 1.0 - omega
        scale = omega * rho
        base = scale * (1.0 - 1.5 * (vel[0] * vel[0] + vel[1] * vel[1] + vel[2] * vel[2]))
        quad_v = [4.5 * scale * v for v in vel]
        lin = [(3.0 * scale) * v for v in vel]
        diag = [quad_v[d] * vel[d] for d in range(3)]
        tail = {0: 0.0, 1: 0.0, 2: 0.0}
        if grads is not None:
            quad_g = [0.5 * inv_mag * g for g in grads]
            diag = [diag[d] + quad_g[d] * grads[d] for d in range(3)]
            tail = {
                0: (1.0 / 9.0) * mag,
                1: (-0.5 / 54.0) * mag,
                2: (-0.5 / 27.0) * mag,
            }

        def cross(a, b):
            total = quad_v[a] * vel[b]
            if grads is not None:
                total = total + quad_g[a] * grads[b]
            return 2.0 * total

        memo = {}

        def once(key, make):
            if key not in memo:
                memo[key] = make()
            return memo[key]

        for member in pops:
            if member >= NF:
                continue
            dims = [d for d in range(3) if VEL[member][d] != 0]
            signs = [VEL[member][d] for d in dims]
            if not dims:
                out[member] = keep * pops[member] + ((1.0 / 3.0) * base + tail[0])
                continue
            if len(dims) == 1:
                d = dims[0]
                even = once(("e", d), lambda: (1.0 / 18.0) * (base + diag[d]) + tail[1])
                odd = once(("o", d), lambda: (1.0 / 18.0) * lin[d])
                flip = signs[0]
            else:
                a, b = dims
                same = signs[0] * signs[1]
                both = once(("s", a, b), lambda: base + diag[a] + diag[b])
                mixed = once(("m", a, b), lambda: cross(a, b))
                even = once(
                    ("e", a, b, same),
                    lambda: (1.0 / 36.0) * (both + mixed if same > 0 else both - mixed) + tail[2],
                )
                odd = once(
                    ("o", a, b, same),
                    lambda: (1.0 / 36.0) * (lin[a] + lin[b] if same > 0 else lin[a] - lin[b]),
                )
                flip = signs[0]
            mid = keep * pops[member] + even
            out[member] = mid + odd if flip > 0 else mid - odd
    if any(member >= NF for member in pops):
        part = 1.25 * 0.125
        if grads is not None:
            sharpen = 0.7 * (1.0 - phase * phase) * inv_mag
        for member in pops:
            if member < NF:
                continue
            move = VEL[member]
            if move == (0, 0, 0):
                out[member] = (1.25 * 0.25) * phase - 0.25 * pops[member]
                continue
            d = [i for i in range(3) if move[i] != 0][0]
            drift = 4.0 * phase * vel[d]
            if grads is not None:
                drift = drift + sharpen * grads[d]
            still = part * phase - 0.25 * pops[member]
            out[member] = still + part * drift if move[d] > 0 else still - part * drift
    return out


def relax_rest(phase, grads, pops):
    square = grads[0] * grads[0] + grads[1] * grads[1] + grads[2] * grads[2] + 0.01
    inv_mag = lax.rsqrt(square)
    mag = square * inv_mag
    half = 0.5 * inv_mag
    sharpen = (1.25 * 0.125 * 0.7) * (1.0 - phase * phase) * inv_mag
    quad = [half * g for g in grads]
    diag = [quad[d] * grads[d] for d in range(3)]
    memo = {}
    out = {}
    for member in pops:
        move = VEL[member]
        dims = [d for d in range(3) if move[d] != 0]
        if member >= NF:
            if dims:
                d = dims[0]
                if d not in memo:
                    memo[d] = sharpen * grads[d]
                out[member] = pops[member] + memo[d] if move[d] > 0 else pops[member] - memo[d]
            else:
                out[member] = pops[member]
            continue
        key = tuple(abs(v) for v in move) + (
            (move[dims[0]] * move[dims[1]],) if len(dims) == 2 else ()
        )
        if key not in memo:
            if not dims:
                memo[key] = (1.0 / 9.0) * mag
            elif len(dims) == 1:
                memo[key] = (1.0 / 18.0) * diag[dims[0]] - (0.5 / 54.0) * mag
            else:
                a, b = dims
                mixed = 2.0 * (quad[a] * grads[b])
                both = diag[a] + diag[b]
                both = both + mixed if key[3] > 0 else both - mixed
                memo[key] = (1.0 / 36.0) * both - (0.5 / 27.0) * mag
        out[member] = pops[member] + memo[key]
    return out


def moments(pops):
    rho = pops[0]
    for member in range(1, NF):
        rho = rho + pops[member]
    mom = []
    for d in range(3):
        plus = [pops[m] for m in range(NF) if VEL[m][d] > 0]
        minus = [pops[m] for m in range(NF) if VEL[m][d] < 0]
        total = plus[0] - minus[0]
        for p, m in zip(plus[1:], minus[1:]):
            total = total + (p - m)
        mom.append(total)
    return rho, mom


def add_up(values):
    total = values[0]
    for value in values[1:]:
        total = total + value
    return total


def turn(value, shift, dim):
    size = value.shape[dim]
    shift = shift % size
    return pltpu.roll(value, shift, axis=dim) if shift else value


def load_kernel(flow, phase, mask, own, cells, ends, out_a, out_b, mask_in, sem):
    _, cx, cy, cz = own.shape
    copies = [
        pltpu.make_async_copy(flow, own.at[pl.ds(0, NF)], sem.at[0]),
        pltpu.make_async_copy(phase, own.at[pl.ds(NF, NG)], sem.at[1]),
        pltpu.make_async_copy(mask, mask_in, sem.at[2]),
    ]
    for one in copies:
        one.start()
    for one in copies:
        one.wait()
    cells[NP] = mask_in[...].astype(jnp.float32)
    for x in range(cx):
        values = [own[member, x] for member in range(NP)]
        rho, mom = moments(values)
        done = relax(rho, mom, add_up(values[NF:]), None, dict(enumerate(values)))
        for member in range(NP):
            cells[member, x] = done[member]
    even = lax.axis_index("gz") % 2 == 0
    lane = lax.broadcasted_iota(jnp.int32, (cy, cz), 1)
    group = lane // (2 * HALO)
    first_half = lane % (2 * HALO) < HALO
    per = cz // (2 * HALO * cx)
    for block in range(ends.shape[0]):
        total = jnp.zeros((cy, cz), jnp.float32)
        for field in range(block * per, min((block + 1) * per, NV)):
            for x in range(cx):
                slot = (field % per) * cx + x
                value = turn(cells[field, x], slot * 2 * HALO + HALO, 1)
                total = jnp.where(group == slot, value, total)
        ends[block] = total
    for pair in range(out_a.shape[0]):
        one = ends[2 * pair]
        two = ends[min(2 * pair + 1, ends.shape[0] - 1)]
        high = jnp.where(first_half, one, turn(two, HALO, 1))
        low = jnp.where(first_half, turn(one, -HALO, 1), two)
        out_a[pair] = jnp.where(even, high, low)
        out_b[pair] = jnp.where(even, low, high)


def pack_face(own, out, base, up):
    cx = own.shape[1]
    other = jnp.where(up, 0, 1)
    xs = [jnp.where(up, cx - 1 - d, d) for d in range(HALO)]
    for field in range(NV):
        out[base + field] = own[field, xs[0]]
    base = base + NV
    for member in range(NG):
        out[base + L_G2 + member] = own[NF + member, xs[1]]
    for slot, member in enumerate(IN_F):
        out[base + L_F2 + slot] = own[member + other, xs[1]]
    out[base + L_G3] = own[NF + IN_G + other, xs[2]]
    out[base + L_PH3] = add_up([own[NF + member, xs[2]] for member in range(NG)])
    far = add_up([own[NF + member, xs[3]] for member in range(NG)])
    out[base + L_PH4] = jnp.where(own[NP, xs[3]] == 1.0, far, 0.0)
    for d in range(2):
        out[base + L_MASK + d] = own[NP, xs[1 + d]]


def faces_kernel(own, out_a, out_b):
    even = lax.axis_index("gx") % 2 == 0
    pack_face(own, out_a, 0, even)
    pack_face(own, out_b, 0, jnp.logical_not(even))


def merged(cx, cz):
    return NF // (cz // (2 * HALO * cx)) // 2


def strips_kernel(ends, z_a, z_b, strips, out_a, out_b, *, sizes, cx):
    blocks, cy, cz = ends.shape
    at_z = lax.axis_index("gz")
    even = at_z % 2 == 0
    lane = lax.broadcasted_iota(jnp.int32, (cy, cz), 1)
    first_half = lane % (2 * HALO) < HALO
    has_below = at_z > 0
    has_above = at_z < sizes["gz"] - 1
    for block in range(blocks):
        from_a, from_b = z_a[block // 2], z_b[block // 2]
        below = jnp.where(even, from_b, from_a)
        above = jnp.where(even, from_a, from_b)
        if block % 2 == 0:
            above = turn(above, HALO, 1)
        else:
            below = turn(below, -HALO, 1)
        if block == blocks - 1:
            below = jnp.where(has_below, below, 0.0)
            above = jnp.where(has_above, above, 0.0)
        own = ends[block]
        strips[block] = jnp.where(first_half, below, own)
        strips[blocks + block] = jnp.where(first_half, own, above)

    wide = 2 * HALO * cx
    pairs = merged(cx, cz)
    even_x = lax.axis_index("gx") % 2 == 0
    count = out_a.shape[0] // 2
    upper = lane % wide >= wide // 2
    for out, up in ((out_a, even_x), (out_b, jnp.logical_not(even_x))):
        near = upper == up
        shift = jnp.where(up, cz - wide // 2, wide // 2)
        for side in range(2):
            for pair in range(pairs):
                one = strips[side * blocks + 2 * pair]
                two = pltpu.roll(strips[side * blocks + 2 * pair + 1], shift, axis=1)
                out[side * count + pair] = jnp.where(near, one, two)
            for block in range(2 * pairs, blocks):
                out[side * count + block - pairs] = strips[side * blocks + block]


def steps_kernel(
    own, cells, cells_y, strips, strips_y, far_a, far_b, far_a_y, far_b_y,
    x_a, x_b, x_a_y, x_b_y,
    flow_out, phase_out,
    face, fluid, potential,
    strip_pops, strip_fluid, fill_moved, fill_moved1, moved, stayed, strip_moved, strip_stayed,
    phase_pops, potential1, moved1, stayed1, result, sem,
    *, sizes,
):
    _, cx, cy, cz = own.shape
    rows = 2 * cy
    at_x = lax.axis_index("gx")
    at_y = lax.axis_index("gy")
    even_x = at_x % 2 == 0
    first, last = HALO, HALO + cx - 1
    own_rows = pl.ds(0, cy)

    def whole(cells, cells_y, *at):
        return jnp.concatenate([cells[at], cells_y[at]], axis=0)

    both = pl.ds(cy, rows)

    def put(ref, at, value):
        ref[(*at, both)] = value
        ref[(*at, own_rows)] = value[cy:]

    def rows_from(step, half):
        if half == 0:
            return pl.ds(cy - step, cy)
        return pl.ds(1, cy) if step < 0 else pl.ds(rows - step, cy)

    def take(ref, at, step):
        return jnp.concatenate([ref[(*at, rows_from(step, half))] for half in (0, 1)], axis=0)

    lane = lax.broadcasted_iota(jnp.int32, (rows, cz), 1)
    row = lax.broadcasted_iota(jnp.int32, (rows, cz), 0)
    has_left = at_x > 0
    has_right = at_x < sizes["gx"] - 1
    has_low = at_y > 0
    has_high = at_y < sizes["gy"] - 1
    high_row = jnp.where(has_high, cy + HALO, cy)
    low_row = jnp.where(has_low, cy + HALO, rows)
    row_ok = (row < high_row) | (row >= low_row)
    has = (has_left, has_right)

    def at_depth(side, depth):
        return first - depth if side == 0 else last + depth

    side_a = jnp.where(even_x, 1, 0)
    ends = ((x_a, x_a_y, side_a), (x_b, x_b_y, 1 - side_a))

    def whole_face(end, layer):
        return whole(end[0], end[1], layer)

    for x in range(cx):
        ok = (whole(cells, cells_y, NP, x) == 1.0) & row_ok
        fluid[first + x] = ok.astype(jnp.float32)
        total = add_up([whole(cells, cells_y, NF + member, x) for member in range(NG)])
        put(potential, (first + x,), jnp.where(ok, total, 0.0))
    for end in ends:
        side = end[2]
        for layer in range(N_FACE):
            face[side, layer] = whole_face(end, NV + layer)
        at = jnp.where(side == 0, first - 1, last + 1)
        side_ok = row_ok & ((side == 0) & has_left | (side == 1) & has_right)
        ok = side_ok & (whole_face(end, NP) == 1.0)
        total = add_up([whole_face(end, NF + member) for member in range(NG)])
        fluid[at] = ok.astype(jnp.float32)
        put(potential, (at,), jnp.where(ok, total, 0.0))
    for side in range(2):
        side_ok = row_ok & has[side]
        for depth in range(2, HALO + 1):
            at = at_depth(side, depth)
            ok = side_ok
            if depth == 2:
                total = add_up([face[side, L_G2 + m] for m in range(NG)])
            else:
                total = face[side, L_PH3 if depth == 3 else L_PH4]
            if depth < HALO:
                ok = ok & (face[side, L_MASK + depth - 2] == 1.0)
                fluid[at] = ok.astype(jnp.float32)
            put(potential, (at,), jnp.where(ok, total, 0.0))

    cols = 2 * HALO
    wide = cols * cx
    per = cz // wide
    block_ok = row_ok & (
        ((lane < wide) & has_left)
        | ((lane >= wide) & (lane < 2 * wide))
        | ((lane >= 2 * wide) & (lane < 3 * wide) & has_right)
    )
    blocks = strips.shape[0] // 2
    count = far_a.shape[0] // 2
    pairs = merged(cx, cz)
    group = lane // wide
    for side in range(2):
        for block in range(blocks):
            second = block < 2 * pairs and block % 2
            at = side * count + (block // 2 if block < 2 * pairs else block - pairs)
            from_a = whole(far_a, far_a_y, at)
            from_b = whole(far_b, far_b_y, at)
            left = jnp.where(even_x, from_b, from_a)
            right = jnp.where(even_x, from_a, from_b)
            left = turn(left, wide // 2 if second else 0, 1)
            right = turn(right, 2 * wide - (wide // 2 if second else 0), 1)
            mine = turn(whole(strips, strips_y, side * blocks + block), wide, 1)
            for field in range(block * per, min((block + 1) * per, NV)):
                spot = field % per
                value = jnp.where(
                    group == spot, left, jnp.where(group == (spot + 1) % per, mine, right)
                )
                value = turn(value, -spot * wide, 1)
                if field < NP:
                    strip_pops[side, field] = value
                else:
                    strip_fluid[side] = jnp.where(block_ok, value, 0.0)

    def strip_grads(values):
        return (
            0.5 * (turn(values, -cols, 1) - turn(values, cols, 1)),
            0.5 * (turn(values, -1, 0) - turn(values, 1, 0)),
            0.5 * (turn(values, -1, 1) - turn(values, 1, 1)),
        )

    def push_strip(member, value, ok):
        move = VEL[member]
        value = jnp.where(ok, value, ROCK)
        return turn(value, move[0] * cols + move[2], 1)

    from_low = lane % cols == HALO
    fills = {}
    for member in range(NP):
        if VEL[member][2] > 0:
            base = 0 if member < NF else NF
            move = VEL[member]
            twin = base + VEL_F.index((move[0], move[1], -1))
            fills[member] = fills[twin] = (len(fills) // 2, member, twin)

    def to_ends(values, at):
        return pltpu.roll(values, (2 * cz - (at * cols + HALO)) % cz, axis=1)

    def main_grads(source, fill, at):
        here = source[at, both]
        fill = to_ends(fill, at)
        down = jnp.where(lane == 0, fill, turn(here, 1, 1))
        up = jnp.where(lane == cz - 1, fill, turn(here, -1, 1))
        return (
            0.5 * (source[at + 1, both] - source[at - 1, both]),
            0.5 * (take(source, (at,), -1) - take(source, (at,), 1)),
            0.5 * (up - down),
        )

    def push_z(member, value, source, at, part, memo):
        move = VEL[member]
        if move[2] == 0:
            return value
        size = value.shape[0]
        number = fills[member][0]
        if number not in memo:
            memo[number] = to_ends(source[number, part], at + move[0])
        edge = 0 if move[2] > 0 else cz - 1
        return jnp.where(lane[:size] == edge, memo[number], turn(value, move[2], 1))

    def push_main(member, value, ok, at, memo):
        value = jnp.where(ok, value, ROCK)
        value = push_z(member, value, fill_moved, at, pl.ds(0, rows), memo)
        if VEL[member][1]:
            put(moved, (member, at), value)
        else:
            moved[member, at, both] = value

    totals = []
    for side in range(2):
        ok = strip_fluid[side] == 1.0
        values = [strip_pops[side, member] for member in range(NP)]
        total = jnp.where(ok, add_up(values[NF:]), 0.0)
        totals.append(turn(total, 1 if side == 0 else -1, 1))
        done = relax_rest(total, strip_grads(total), dict(enumerate(values)))
        for member in range(NP):
            strip_stayed[side, member] = done[member]
            put(strip_moved, (side, member), push_strip(member, done[member], ok))

    fill_phase = jnp.where(from_low, totals[0], totals[1])
    for number, low, high in sorted(set(fills.values())):
        fill_moved[number] = jnp.where(
            from_low, strip_moved[0, low, both], strip_moved[1, high, both]
        )

    def collide(at, values):
        ok = fluid[at] == 1.0
        grads = main_grads(potential, fill_phase, at)
        done = relax_rest(potential[at, both], grads, dict(enumerate(values)))
        memo = {}
        for member in range(NP):
            stayed[member, at] = done[member]
            push_main(member, done[member], ok, at, memo)

    def collide_own(x, carry):
        collide(first + x, [whole(cells, cells_y, member, x) for member in range(NP)])
        return carry

    lax.fori_loop(0, cx, collide_own, 0, unroll=2)
    for end in ends:
        collide(
            jnp.where(end[2] == 0, first - 1, last + 1),
            [whole_face(end, member) for member in range(NP)],
        )
    for side in range(2):
        at = at_depth(side, 2)
        members = {m + side: face[side, L_F2 + slot] for slot, m in enumerate(IN_F)}
        members.update({NF + m: face[side, L_G2 + m] for m in range(NG)})
        done = relax_rest(potential[at, both], main_grads(potential, fill_phase, at), members)
        ok = fluid[at] == 1.0
        memo = {}
        for member in done:
            stayed[member, at] = done[member]
            push_main(member, done[member], ok, at, memo)
        at = at_depth(side, 3)
        member = NF + IN_G + side
        done = relax_rest(
            potential[at, both], main_grads(potential, fill_phase, at),
            {member: face[side, L_G3]},
        )
        ok = fluid[at] == 1.0
        push_main(member, done[member], ok, at, {})

    def pull(member, at, half):
        part = pl.ds(half * cy, cy)
        if VEL[member] == (0, 0, 0):
            return stayed[member, at, part]
        move = VEL[member]
        value = moved[member, at - move[0], rows_from(move[1], half)]
        return jnp.where(value == ROCK, stayed[OPP[member], at, part], value)

    def stream(j, carry):
        at = first - 2 + j
        values = [
            jnp.concatenate([pull(NF + member, at, half) for half in (0, 1)], axis=0)
            for member in range(NG)
        ]
        for member in range(NG):
            phase_pops[member, at] = values[member]
        put(potential1, (at,), jnp.where(fluid[at] == 1.0, add_up(values), 0.0))
        return carry

    lax.fori_loop(0, cx + 4, stream, 0, unroll=2)

    totals = []
    crossed = {}
    for side in range(2):
        ok = strip_fluid[side] == 1.0
        values = []
        for member in range(NP):
            value = take(strip_moved, (side, member), VEL[member][1])
            back = strip_stayed[side, OPP[member]]
            values.append(jnp.where(value == ROCK, back, value))
        total = jnp.where(ok, add_up(values[NF:]), 0.0)
        rho, mom = moments(values)
        sign = 1 if side == 0 else -1
        wanted = {m: values[m] for m in range(NP) if VEL[m][2] == sign}
        done = relax(rho, mom, total, strip_grads(total), wanted)
        for member in wanted:
            crossed[member] = push_strip(member, done[member], ok)
        totals.append(turn(total, sign, 1))
    fill_phase1 = jnp.where(from_low, totals[0], totals[1])
    for number, low, high in sorted(set(fills.values())):
        fill_moved1[number] = jnp.where(from_low, crossed[low], crossed[high])

    def collide1(at, wanted, keep):
        grads = main_grads(potential1, fill_phase1, at)
        halves = []
        for half in range(2):
            part = pl.ds(half * cy, cy)
            values = [pull(member, at, half) for member in range(NF)]
            values += [phase_pops[member, at, part] for member in range(NG)]
            rho, mom = moments(values)
            members = [m for m in wanted if half == 0 or VEL[m][1] != 0]
            done = relax(
                rho, mom, potential1[at, pl.ds((1 + half) * cy, cy)],
                [g[half * cy : (half + 1) * cy] for g in grads],
                {m: values[m] for m in members},
            )
            halves.append((done, fluid[at, part] == 1.0))
        (done, ok), (done_y, ok_y) = halves
        memo, memo_y = {}, {}
        for member in wanted:
            if keep:
                stayed1[member, at] = done[member]
            value = jnp.where(ok, done[member], ROCK)
            middle = pl.ds(cy, cy)
            moved1[member, at, middle] = push_z(member, value, fill_moved1, at, own_rows, memo)
            if VEL[member][1]:
                beyond = pl.ds(0, cy) if VEL[member][1] > 0 else pl.ds(rows, cy)
                value = jnp.where(ok_y, done_y[member], ROCK)
                moved1[member, at, beyond] = push_z(
                    member, value, fill_moved1, at, pl.ds(cy, cy), memo_y
                )

    def outputs(x):
        return (
            pltpu.make_async_copy(
                result.at[pl.ds(0, NF), x], flow_out.at[:, x], sem.at[0, x]
            ),
            pltpu.make_async_copy(
                result.at[pl.ds(NF, NG), x], phase_out.at[:, x], sem.at[1, x]
            ),
        )

    def finish(x):
        at = first + x
        ok = fluid[at, own_rows] == 1.0
        for member in range(NP):
            if VEL[member] == (0, 0, 0):
                value = stayed1[member, at]
            else:
                move = VEL[member]
                value = moved1[member, at - move[0], pl.ds(cy - move[1], cy)]
                value = jnp.where(value == ROCK, stayed1[OPP[member], at], value)
            result[member, x] = jnp.where(ok, value, own[member, x])
        for one in outputs(x):
            one.start()

    collide1(first - 1, [m for m in range(NP) if VEL[m][0] == 1], False)
    for x in range(cx):
        collide1(first + x, range(NP), True)
        if x > 0:
            finish(x - 1)
    collide1(last + 1, [m for m in range(NP) if VEL[m][0] == -1], False)
    finish(cx - 1)
    for x in range(cx):
        for one in outputs(x):
            one.wait()


def shards(sizes, flow_pops, phase_pops, pore_mask):
    cx, cy, cz = pore_mask.shape
    rows = 2 * cy
    assert cx >= HALO and cy == 2 * HALO and 6 * cx * HALO <= cz
    f32 = jnp.float32
    vmem = pl.BlockSpec(memory_space=pltpu.VMEM)
    anywhere = pl.BlockSpec(memory_space=pl.ANY)

    def near(*arrays):
        return [pltpu.with_memory_space_constraint(a, pltpu.VMEM) for a in arrays]

    def call(kernel, out_shape, in_specs, args, scratch=(), out_specs=None):
        return pl.pallas_call(
            kernel,
            out_shape=out_shape,
            in_specs=in_specs,
            out_specs=out_specs or jax.tree.map(lambda _: vmem, out_shape),
            scratch_shapes=scratch,
        )(*args)

    end_blocks = pl.cdiv(NV, cz // (2 * HALO * cx))
    end_shape = pltpu.VMEM((end_blocks, cy, cz), f32)
    z_shape = pltpu.VMEM((pl.cdiv(end_blocks, 2), cy, cz), f32)
    own, cells, ends, z_a, z_b = call(
        load_kernel,
        (
            pltpu.VMEM((NP, cx, cy, cz), f32),
            pltpu.VMEM((NV, cx, cy, cz), f32),
            end_shape,
            z_shape,
            z_shape,
        ),
        [anywhere] * 3, (flow_pops, phase_pops, pore_mask),
        [
            pltpu.VMEM(pore_mask.shape, jnp.int32),
            pltpu.SemaphoreType.DMA((3,)),
        ],
    )
    cells_y = beside(sizes, cells)
    z_a, z_b = swap(sizes, "gz", z_a, z_b)

    x_shape = pltpu.VMEM((NV + N_FACE, cy, cz), f32)
    x_a, x_b = call(faces_kernel, (x_shape, x_shape), [vmem], near(cells))
    x_a, x_b = swap(sizes, "gx", x_a, x_b)
    x_a_y = beside(sizes, x_a)
    x_b_y = beside(sizes, x_b)

    strip_blocks = 2 * end_blocks
    far_shape = pltpu.VMEM((strip_blocks - 2 * merged(cx, cz), cy, cz), f32)
    strips, far_a, far_b = call(
        lambda *refs: strips_kernel(*refs, sizes=sizes, cx=cx),
        (pltpu.VMEM((strip_blocks, cy, cz), f32), far_shape, far_shape),
        [vmem] * 3, near(ends, z_a, z_b),
    )
    strips_y = beside(sizes, strips)
    far_a, far_b = swap(sizes, "gx", far_a, far_b)
    far_a_y = beside(sizes, far_a)
    far_b_y = beside(sizes, far_b)

    deep = cx + 2 * HALO

    def block(*lead):
        return pltpu.VMEM((*lead, rows, cz), f32)

    def tall(*lead):
        return pltpu.VMEM((*lead, rows + cy, cz), f32)

    return call(
        lambda *refs: steps_kernel(*refs, sizes=sizes),
        (
            jax.ShapeDtypeStruct(flow_pops.shape, f32),
            jax.ShapeDtypeStruct(phase_pops.shape, f32),
        ),
        [vmem] * 13,
        near(
            own, cells, cells_y, strips, strips_y, far_a, far_b, far_a_y, far_b_y,
            x_a, x_b, x_a_y, x_b_y,
        ),
        [
            block(2, N_FACE),
            block(deep),
            tall(deep),
            block(2, NP),
            block(2),
            block(6),
            block(6),
            tall(NP, deep),
            block(NP, deep),
            tall(2, NP),
            block(2, NP),
            block(NG, deep),
            tall(deep),
            tall(NP, deep),
            pltpu.VMEM((NP, deep, cy, cz), f32),
            pltpu.VMEM((NP, cx, cy, cz), f32),
            pltpu.SemaphoreType.DMA((2, cx)),
        ],
        (anywhere, anywhere),
    )


def solution(mesh):
    sizes = dict(mesh.shape)
    placed = (P(None, "gx", "gy", "gz"), P(None, "gx", "gy", "gz"), P("gx", "gy", "gz"))
    return jax.shard_map(
        lambda *args: shards(sizes, *args),
        mesh=mesh,
        in_specs=placed,
        out_specs=(P(None, "gx", "gy", "gz"), P(None, "gx", "gy", "gz")),
        check_vma=False,
    )
```
